128 devices in a mesh: dp: 4 (over y), mp: 32 (over x, z, core).
Axes of the slice: x: 4, y: 4, z: 4, core: 2. Of those that a mesh axis runs over, the one named last changes fastest.
Arguments:
- inputs: bfloat16 [2048, 4096], P('dp'), may hold values from -6 to 6
- out_grads: bfloat16 [2048, 4096], P('dp'), may hold values from -0.3984375 to 0.3984375
- w_gate: bfloat16 [4096, 11008], P(None, 'mp'), may hold values from -0.09375 to 0.09375
- w_up: bfloat16 [4096, 11008], P(None, 'mp'), may hold values from -0.09375 to 0.09375
- w_down: bfloat16 [11008, 4096], P('mp'), may hold values from -0.0546875 to 0.0546875
- err_down: bfloat16 [4, 11008, 4096], P('dp', 'mp'), may hold values from -3 to 3
- mom_down: float32 [11008, 4096], P('mp', 'dp'), may hold values from -0.3 to 0.3
- q_down: float32 [4096, 8], replicated, may hold values from -5 to 5
Outputs:
- in_grads: bfloat16 [2048, 4096], P('dp', 'mp')
- new_down: bfloat16 [11008, 4096], P('mp')
- next_err_down: bfloat16 [4, 11008, 4096], P('dp', 'mp')
- next_mom_down: float32 [11008, 4096], P('mp', 'dp')
The draws below stay inside these ranges and needn't reach their ends.
All inputs are finite; a program needn't handle non-finite values.
Results may differ from the reference program's by a relative error of at most 0.005.
Values may be sent and summed in bfloat16 or wider, within the bound.
A program may use at most 128 MiB of HBM per device.

```python
import jax
import jax.numpy as jnp
from jax import lax

D = 4096
FF = 11008
TOK = 512
R = 8
TOKENS = 2048
N_DP = 4


def shard_levels(own_key, extent, pieces, low, high):
    def one(axis_at, blocks):
        draws = jax.random.uniform(jax.random.fold_in(jax.random.fold_in(own_key, 6), axis_at), (blocks,), jnp.float32, low / len(pieces), high / len(pieces))
        return jnp.repeat(jnp.exp(draws), extent[axis_at] // blocks).reshape((-1,) + (1,) * (len(extent) - axis_at - 1))

    factor_of = one(*pieces[0])
    for cut in pieces[1:]:
        factor_of = factor_of * one(*cut)
    return factor_of


def gaussian(stream_key, dims, spread, most, pieces=(), dtype=jnp.bfloat16):
    array = jax.random.normal(stream_key, dims, jnp.float32) * spread
    if len(pieces) > 0:
        array = shard_levels(stream_key, dims, pieces, -0.22, 0.18) * array
    return jnp.clip(array, min=-most, max=most).astype(dtype)


def setup_inputs(seed: int = 0) -> dict:
    splits = jax.random.split(jax.random.key(seed), 9)
    return {
        "inputs": gaussian(splits[0], (TOKENS, D), 1.0, 6.0, ((0, 4),)),
        "out_grads": gaussian(splits[1], (TOKENS, D), 0.0625, 0.3984375, ((0, 4),)),
        "w_gate": gaussian(splits[2], (D, FF), D ** -0.5, 0.09375, ((1, 32),)),
        "w_up": gaussian(splits[3], (D, FF), D ** -0.5, 0.09375, ((1, 32),)),
        "w_down": gaussian(splits[4], (FF, D), FF ** -0.5, 0.0546875, ((0, 32),)),
        "err_down": gaussian(splits[5], (N_DP, FF, D), 0.5, 3.0, ((0, 4), (1, 32))),
        "mom_down": gaussian(splits[6], (FF, D), 0.05, 0.3, ((0, 32), (1, 4)), jnp.float32),
        "q_down": gaussian(splits[7], (D, R), 1.0, 5.0, (), jnp.float32),
    }


HIGH = lax.Precision.HIGHEST

def orthonormal(panel):
    finished = []
    for col in range(R):
        vector = panel[:, col]
        if col > 0:
            basis = jnp.stack(finished, 1)
            coeffs = jnp.dot(basis.T, vector, precision=HIGH)
            vector = vector - jnp.dot(basis, coeffs, precision=HIGH)
        vector = vector * lax.rsqrt(jnp.sum(vector * vector) + 1e-06)
        finished.append(vector)
    return jnp.stack(finished, 1)

def compress(corrected, right):
    left = sum((jnp.dot(m, right, precision=HIGH) for m in corrected)) / N_DP
    left = orthonormal(left)
    right_new = sum((jnp.dot(m.T, left, precision=HIGH) for m in corrected)) / N_DP
    return jnp.dot(left, right_new.T, precision=HIGH)

def reference(inputs, out_grads, w_gate, w_up, w_down, err_down, mom_down, q_down):
    in_rows = []
    m_down = []
    for rep in range(N_DP):
        x_rows = inputs[rep * TOK:(rep + 1) * TOK]
        dy_rows = out_grads[rep * TOK:(rep + 1) * TOK]
        gate = jnp.dot(x_rows, w_gate, preferred_element_type=jnp.float32)
        up_val = jnp.dot(x_rows, w_up, preferred_element_type=jnp.float32)
        sig = jax.nn.sigmoid(gate)
        hidden = (gate * sig * up_val).astype(jnp.bfloat16)
        d_hidden = jnp.dot(dy_rows, w_down.T, preferred_element_type=jnp.float32)
        d_gate = (d_hidden * up_val * sig * (1.0 + gate * (1.0 - sig))).astype(jnp.bfloat16)
        d_up = (d_hidden * gate * sig).astype(jnp.bfloat16)
        part = jnp.dot(d_gate, w_gate.T, preferred_element_type=jnp.float32) + jnp.dot(d_up, w_up.T, preferred_element_type=jnp.float32)
        in_rows.append(part.astype(jnp.bfloat16))
        m_down.append(jnp.dot(hidden.T, dy_rows, preferred_element_type=jnp.float32) + err_down[rep].astype(jnp.float32))
    approx = compress(m_down, q_down)
    errors = jnp.stack([(m - approx).astype(jnp.bfloat16) for m in m_down], 0)
    mom_next = 0.9 * mom_down + approx
    weight_next = (w_down.astype(jnp.float32) - 0.1 * mom_next).astype(jnp.bfloat16)
    return (jnp.concatenate(in_rows, 0), weight_next, errors, mom_next)
```

```python
import functools

import jax
import jax.numpy as jnp
from jax import lax
from jax.experimental import pallas as pl
from jax.experimental.pallas import tpu as pltpu
from jax.sharding import PartitionSpec as P

MESH = pl.DeviceIdType.MESH
BF = jnp.bfloat16
F32 = jnp.float32
TOK, D, F, FP, R = 512, 4096, 344, 384, 8
KC = 1024
NK = D // KC
N_SEM = 128


def nt(a, b):
    return lax.dot_general(a, b, (((1,), (1,)), ((), ())), preferred_element_type=F32)


def nn(a, b):
    return lax.dot_general(a, b, (((1,), (0,)), ((), ())), preferred_element_type=F32)


def split3(v):
    hi = v.astype(BF).astype(F32)
    rest = v - hi
    mid = rest.astype(BF).astype(F32)
    low = rest - mid
    return jnp.concatenate([hi, mid, low, jnp.zeros_like(v)], axis=0).astype(BF)


def fold(r):
    return (r[0:8] + r[8:16]) + r[16:24]


def step_kernel(
    x_h, dy_h, wg_h, wu_h, wd_h, er_h, mo_h, q_h,
    ig_o, tg_o, m_o, sf_o, tt_o, pf_o,
    xs, dys, wgs, wus, wds, ers, mos, qs,
    wgp, wup, g, u, dh, hs, ht, dg, du, dgp, dup, ts, ms, q3,
    dyq, erq, pown, py_r, p3, pg, ct,
    sb, sc_r, sx_r, s1, sz_r, s2, sy_r, sf, tt, pf,
    rs_p, ra_r, rb_r, a1, b1, za_r, xb_r, igs,
    load_sem, send_sem, recv_sem,
):
    dp = lax.axis_index("dp")
    mp = lax.axis_index("mp")
    core = lax.rem(mp, 2)
    z = lax.rem(mp // 2, 4)
    x = mp // 8
    other = 1 - core

    def wrap(v):
        return lax.rem(v, 4)

    to_core = (dp, mp + 1 - 2 * core)

    def to_x(d):
        return (dp, wrap(x + d) * 8 + z * 2 + core)

    def to_z(d):
        return (dp, x * 8 + wrap(z + d) * 2 + core)

    def to_y(d):
        return (wrap(dp + d), mp)

    barrier = pltpu.get_barrier_semaphore()
    peers = [to_core] + [f(d) for f in (to_x, to_z, to_y) for d in (1, 2, 3)]
    for peer in peers:
        pl.semaphore_signal(barrier, inc=1, device_id=peer, device_id_type=MESH)

    def lx(k):
        return pltpu.make_async_copy(x_h.at[:, pl.ds(k * KC, KC)], xs.at[k], load_sem.at[k])

    def ly(k):
        return pltpu.make_async_copy(dy_h.at[:, pl.ds(k * KC, KC)], dys.at[k], load_sem.at[4 + k])

    def lwd(k):
        return pltpu.make_async_copy(wd_h.at[:, pl.ds(k * KC, KC)], wds.at[k], load_sem.at[8 + k])

    def ler(k):
        return pltpu.make_async_copy(er_h.at[:, pl.ds(k * KC, KC)], ers.at[k], load_sem.at[12 + k])

    def lwg(b):
        return pltpu.make_async_copy(
            wg_h.at[:, pl.ds(b * 128, 128)], wgs.at[b // 2, b % 2], load_sem.at[18 + b]
        )

    def lwu(b):
        return pltpu.make_async_copy(
            wu_h.at[:, pl.ds(b * 128, 128)], wus.at[b // 2, b % 2], load_sem.at[50 + b]
        )

    lmo = pltpu.make_async_copy(mo_h, mos, load_sem.at[16])
    lq = pltpu.make_async_copy(q_h, qs, load_sem.at[17])
    for k in range(NK):
        lx(k).start()
        for b in range(8):
            lwg(8 * k + b).start()
            lwu(8 * k + b).start()
    lq.start()
    lmo.start()
    for k in range(NK):
        lwd(k).start()
    for k in range(NK):
        ly(k).start()
    for k in range(NK):
        ler(k).start()

    count = [0]
    sent = []

    def send(src, dst, device):
        i = count[0]
        count[0] += 1
        c = pltpu.make_async_remote_copy(
            src_ref=src, dst_ref=dst, send_sem=send_sem.at[i], recv_sem=recv_sem.at[i],
            device_id=device, device_id_type=MESH,
        )
        c.start()
        sent.append(c)
        return c

    g[...] = jnp.zeros_like(g)
    u[...] = jnp.zeros_like(u)
    dh[...] = jnp.zeros_like(dh)
    dyq[...] = jnp.zeros_like(dyq)
    erq[...] = jnp.zeros_like(erq)
    hs[...] = jnp.zeros_like(hs)
    pown[...] = jnp.zeros_like(pown)
    pf[...] = jnp.zeros_like(pf)

    @pl.loop(0, NK)
    def _(k):
        lx(k).wait()
        for b in range(8):
            lwg(8 * k + b).wait()
            lwu(8 * k + b).wait()
        a = xs[k]
        wg = jnp.concatenate([wgs[4 * k + b // 2, b % 2] for b in range(8)], axis=1)
        g[...] += nt(a, wg)
        wu = jnp.concatenate([wus[4 * k + b // 2, b % 2] for b in range(8)], axis=1)
        u[...] += nt(a, wu)

    pl.semaphore_wait(barrier, len(peers))
    send_wg = send(wgs.at[:, other], wgp, to_core)
    send_wu = send(wus.at[:, other], wup, to_core)

    lmo.wait()
    for k in range(NK):
        lwd(k).wait()
    for p in range(8):
        lanes = pl.ds(p * 128, 128)
        ts[p] = (wds[dp, :, lanes].astype(F32) - 0.1 * (0.9 * mos[:, lanes])).astype(BF)
    own_t = pltpu.make_async_copy(ts, tg_o.at[dp], load_sem.at[82])
    own_t.start()
    right, left = wrap(dp + 1), wrap(dp + 3)
    t_right, t_left, t_far = [], [], []

    def t_slot(s):
        if s < 8:
            t_right.append(send(ts.at[s], tg_o.at[dp, s], to_y(1)))
            t_left.append(send(ts.at[s], tg_o.at[dp, s], to_y(3)))
        if 1 <= s <= 8:
            p = s - 1
            if p % 2 == 0:
                t_right[p].wait_recv()
                t_far.append(send(tg_o.at[left, p], tg_o.at[left, p], to_y(1)))
            else:
                t_left[p].wait_recv()
                t_far.append(send(tg_o.at[right, p], tg_o.at[right, p], to_y(3)))

    t_slot(0)

    lq.wait()
    for k in range(NK):
        q3[k] = split3(qs[:, k * KC : (k + 1) * KC])

    @pl.loop(0, NK)
    def _(k):
        ly(k).wait()
        dh[...] += nt(dys[k], wds[k])
        dyq[...] += nt(q3[k], dys[k])

    @pl.loop(0, NK)
    def _(k):
        ler(k).wait()
        erq[...] += nt(q3[k], ers[k])

    @pl.loop(0, 8)
    def _(i):
        rows = pl.ds(pl.multiple_of(i * 64, 64), 64)
        gv, uv, dv = g[rows, :], u[rows, :], dh[rows, :]
        sig = jax.nn.sigmoid(gv)
        gs = gv * sig
        hs[rows, 0:F] = (gs * uv).astype(BF)
        dg[rows, :] = (dv * uv * sig * (1.0 + gv * (1.0 - sig))).astype(BF)
        du[rows, :] = (dv * gs).astype(BF)

    send_dg = send(dg, dgp, to_core)
    send_du = send(du, dup, to_core)

    pown[:, 0:F] = fold(nn(split3(fold(dyq[...])), hs[:, 0:F])) + fold(erq[...])
    c_py = [send(pown, py_r.at[d - 1], to_y(d)) for d in (1, 2, 3)]
    t_slot(1)

    ht[...] = hs[...].astype(F32).T.astype(BF)

    @pl.loop(0, NK)
    def _(k):
        ms[k] = nn(ht[0:F, :], dys[k]) + ers[k].astype(F32)
        pltpu.make_async_copy(ms.at[k], m_o.at[k], load_sem.at[83 + k]).start()

    for c in c_py:
        c.wait_recv()
    pf[...] = ((pown[...] + py_r[1]) + (py_r[0] + py_r[2])) * 0.25
    base = z * 24 + x * 6 + core * 3
    for c in range(3):
        pg[base + c] = pf[:, c * 128 : (c + 1) * 128]
    c_pgc = send(pg.at[pl.ds(base, 3)], pg.at[pl.ds(base, 3)], to_core)

    p3[...] = split3(pf[...])
    hp3 = split3(fold(nt(p3[...], hs[...])))

    def s_part(c):
        s = fold(nn(hp3, dys[c]) + nn(p3[:, 0:F], ers[c]))
        for j in range(8):
            sb[8 * c + j] = s[:, j * 128 : (j + 1) * 128]

    s_part(2 * other)
    s_part(2 * other + 1)
    c_sc = send(sb.at[pl.ds(16 * other, 16)], sc_r, to_core)
    s_part(2 * core)
    s_part(2 * core + 1)

    c_pgc.wait_recv()
    xy = z * 24 + x * 6
    c_pgx = [send(pg.at[pl.ds(xy, 6)], pg.at[pl.ds(xy, 6)], to_x(d)) for d in (1, 2, 3)]
    c_sc.wait_recv()
    half = pl.ds(16 * core, 16)
    sb[half] = sb[half] + sc_r[...]
    c_sx = [
        send(sb.at[pl.ds(16 * core + 4 * wrap(x + d), 4)], sx_r.at[d - 1], to_x(d))
        for d in (1, 2, 3)
    ]
    t_slot(2)

    send_wg.wait_recv()
    send_wu.wait_recv()
    send_dg.wait_recv()
    send_du.wait_recv()

    @pl.loop(0, 8)
    def _(i):
        a, b = 2 * i, 2 * i + 1
        r = nn(dg[...], jnp.concatenate([wgs[a, core], wgs[b, core]], axis=1))
        r += nn(du[...], jnp.concatenate([wus[a, core], wus[b, core]], axis=1))
        r += nn(dgp[...], jnp.concatenate([wgp[a], wgp[b]], axis=1))
        r += nn(dup[...], jnp.concatenate([wup[a], wup[b]], axis=1))
        rs_p[a] = r[:, 0:128].astype(BF)
        rs_p[b] = r[:, 128:256].astype(BF)

    top, bottom = pl.ds(0, 256), pl.ds(256, 256)
    c_a, c_b = {}, {}

    def bulk(j):
        for d in (1, 3, 2):
            c_a[j, d] = send(
                rs_p.at[wrap(x + d) * 4 + wrap(z + j), top], ra_r.at[d - 1, j], to_x(d)
            )
            c_b[j, d] = send(
                rs_p.at[wrap(x + j) * 4 + wrap(z + d), bottom], rb_r.at[d - 1, j], to_z(d)
            )

    for c in c_sx:
        c.wait_recv()
    s1[...] = (sb[pl.ds(16 * core + 4 * x, 4)] + sx_r[0]) + (sx_r[1] + sx_r[2])
    c_sz = [send(s1.at[wrap(z + d)], sz_r.at[d - 1], to_z(d)) for d in (1, 2, 3)]
    for c in c_pgx:
        c.wait_recv()
    zz = z * 24
    c_pgz = [send(pg.at[pl.ds(zz, 24)], pg.at[pl.ds(zz, 24)], to_z(d)) for d in (1, 2, 3)]
    bulk(1)
    for c in c_sz:
        c.wait_recv()
    s2[...] = (s1[z] + sz_r[0]) + (sz_r[1] + sz_r[2])
    c_sy = [send(s2, sy_r.at[d - 1], to_y(d)) for d in (1, 2, 3)]
    t_slot(3)
    bulk(2)

    for c in c_pgz:
        c.wait_recv()
    for i in range(12):
        ct[:, i] = jnp.transpose(pg[8 * i : 8 * i + 8], (1, 0, 2))
    lane = lax.broadcasted_iota(jnp.int32, (1, 128), 1)
    done_b, done_t = [], []

    def total(v):
        v = jnp.sum(v, axis=0)
        return jnp.sum(jnp.sum(v, axis=0, keepdims=True), axis=1, keepdims=True)

    for k in range(R):
        v = ct[k]
        t = jnp.where(lane == k, 1.0, 0.0)
        coeffs = [total(b * v) for b in done_b]
        for c, b, tb in zip(coeffs, done_b, done_t):
            v = v - c[None] * b
            t = t - c * tb
        scale = lax.rsqrt(total(v * v) + 1e-06)
        done_b.append(v * scale[None])
        done_t.append(t * scale)
        tt[k : k + 1, :] = done_t[-1]

    for c in c_sy:
        c.wait_recv()
    mine = core * 16 + x * 4 + z
    sf[mine] = (s2[...] + sy_r[1]) + (sy_r[0] + sy_r[2])
    c_gz = [send(sf.at[mine], sf.at[mine], to_z(d)) for d in (1, 2, 3)]
    t_slot(4)
    bulk(3)
    for c in c_gz:
        c.wait_recv()
    mx = pl.ds(core * 16 + x * 4, 4)
    c_gx = [send(sf.at[mx], sf.at[mx], to_x(d)) for d in (1, 2, 3)]
    t_slot(5)
    bulk(0)
    for c in c_gx:
        c.wait_recv()
    mc = pl.ds(core * 16, 16)
    c_gc = send(sf.at[mc], sf.at[mc], to_core)

    def first_sums(j):
        for d in (1, 2, 3):
            c_a[j, d].wait_recv()
            c_b[j, d].wait_recv()
        a = rs_p[x * 4 + wrap(z + j), top, :].astype(F32)
        a = (a + ra_r[0, j].astype(F32)) + (ra_r[1, j].astype(F32) + ra_r[2, j].astype(F32))
        b = rs_p[wrap(x + j) * 4 + z, bottom, :].astype(F32)
        b = (b + rb_r[0, j].astype(F32)) + (rb_r[1, j].astype(F32) + rb_r[2, j].astype(F32))
        return a, b

    c_za, c_xb = [], []
    for j in (1, 2, 3):
        t_slot(5 + j)
        a, b = first_sums(j)
        a1[j] = a.astype(BF)
        b1[j] = b.astype(BF)
        c_za.append(send(a1.at[j], za_r.at[j - 1], to_z(j)))
        c_xb.append(send(b1.at[j], xb_r.at[j - 1], to_x(j)))
    a, b = first_sums(0)
    for c in c_za:
        c.wait_recv()
    igs[0:256, :] = (
        (a + za_r[0].astype(F32)) + (za_r[1].astype(F32) + za_r[2].astype(F32))
    ).astype(BF)
    for c in c_xb:
        c.wait_recv()
    igs[256:512, :] = (
        (b + xb_r[0].astype(F32)) + (xb_r[1].astype(F32) + xb_r[2].astype(F32))
    ).astype(BF)

    c_gc.wait_recv()
    outs = [
        pltpu.make_async_copy(igs, ig_o, load_sem.at[87]),
        pltpu.make_async_copy(sf, sf_o, load_sem.at[88]),
        pltpu.make_async_copy(tt, tt_o, load_sem.at[89]),
        pltpu.make_async_copy(pf, pf_o, load_sem.at[90]),
    ]
    for c in outs:
        c.start()
    for p in range(8):
        if p % 2 == 0:
            t_left[p].wait_recv()
        else:
            t_right[p].wait_recv()
    for c in t_far:
        c.wait_recv()
    for c in sent:
        c.wait_send()
    for c in outs:
        c.wait()
    own_t.wait()
    for k in range(NK):
        pltpu.make_async_copy(ms.at[k], m_o.at[k], load_sem.at[83 + k]).wait()


def exchange(x, dy, wg, wu, wd, er, mo, q):
    v = pltpu.VMEM
    any_spec = pl.BlockSpec(memory_space=pl.ANY)
    scratch = [
        v((NK, TOK, KC), BF), v((NK, TOK, KC), BF),
        v((16, 2, F, 128), BF), v((16, 2, F, 128), BF),
        v((NK, F, KC), BF), v((NK, F, KC), BF), v((F, KC), F32), v((R, D), F32),
        v((16, F, 128), BF), v((16, F, 128), BF),
        v((TOK, F), F32), v((TOK, F), F32), v((TOK, F), F32),
        v((TOK, FP), BF), v((FP, TOK), BF),
        v((TOK, F), BF), v((TOK, F), BF), v((TOK, F), BF), v((TOK, F), BF),
        v((8, F, 128), BF), v((NK, F, KC), F32), v((NK, 32, KC), BF),
        v((32, TOK), F32), v((32, F), F32), v((R, FP), F32), v((3, R, FP), F32),
        v((32, FP), BF), v((96, 8, 128), F32), v((8, 12, 8, 128), F32),
        v((32, 8, 128), F32), v((16, 8, 128), F32), v((3, 4, 8, 128), F32),
        v((4, 8, 128), F32), v((3, 8, 128), F32), v((8, 128), F32), v((3, 8, 128), F32),
        v((32, 8, 128), F32), v((8, 128), F32), v((R, FP), F32),
        v((16, TOK, 128), BF), v((3, 4, 256, 128), BF), v((3, 4, 256, 128), BF),
        v((4, 256, 128), BF), v((4, 256, 128), BF), v((3, 256, 128), BF), v((3, 256, 128), BF),
        v((TOK, 128), BF),
        pltpu.SemaphoreType.DMA((96,)),
        pltpu.SemaphoreType.DMA((N_SEM,)),
        pltpu.SemaphoreType.DMA((N_SEM,)),
    ]
    out_shape = (
        jax.ShapeDtypeStruct((TOK, 128), BF),
        jax.ShapeDtypeStruct((4, 8, F, 128), BF),
        jax.ShapeDtypeStruct((NK, F, KC), F32),
        jax.ShapeDtypeStruct((32, 8, 128), F32),
        jax.ShapeDtypeStruct((8, 128), F32),
        jax.ShapeDtypeStruct((R, FP), F32),
    )
    return pl.pallas_call(
        step_kernel,
        out_shape=out_shape,
        in_specs=[any_spec] * 8,
        out_specs=[any_spec] * 6,
        scratch_shapes=scratch,
        compiler_params=pltpu.CompilerParams(
            collective_id=0, has_side_effects=True, vmem_limit_bytes=62 * 1024 * 1024
        ),
        name="exchange",
    )(x, dy, wg, wu, wd, er, mo, q)


def apply_kernel(ig_ref, t_ref, m_ref, mo_ref, sf_ref, tt_ref, pf_ref,
                 igo_ref, nd_ref, ne_ref, nm_ref, left):
    j = pl.program_id(0)
    dp = lax.axis_index("dp")

    @pl.when(j == 0)
    def _():
        igo_ref[...] = ig_ref[...]
        p = jnp.zeros((R, FP), F32)
        for i in range(R):
            p += tt_ref[:, i : i + 1] * pf_ref[i : i + 1, :]
        hi = p.astype(BF).astype(F32)
        rest = p - hi
        mid = rest.astype(BF).astype(F32)
        low = rest - mid
        rows = [hi, hi, mid, hi, low, mid] + [jnp.zeros_like(p)] * 10
        left[...] = jnp.concatenate(rows, axis=0).T.astype(BF)

    def q_rows(s):
        q = jnp.zeros((R, 128), F32)
        for i in range(R):
            q += tt_ref[:, i : i + 1] * s[i : i + 1, :]
        q = q * 0.25
        hi = q.astype(BF).astype(F32)
        rest = q - hi
        mid = rest.astype(BF).astype(F32)
        low = rest - mid
        rows = [hi, mid, hi, low, hi, mid] + [jnp.zeros_like(q)] * 10
        return jnp.concatenate(rows, axis=0).astype(BF)

    right = jnp.concatenate([q_rows(sf_ref[4 * j + c]) for c in range(4)], axis=1)
    approx = nn(left[0:F, :], right)
    ne_ref[...] = (m_ref[0] - approx).astype(BF)
    for c in range(4):
        lanes = slice(c * 128, (c + 1) * 128)
        nd_ref[:, lanes] = (t_ref[0, c].astype(F32) - 0.1 * approx[:, lanes]).astype(BF)
    nm_ref[...] = 0.9 * mo_ref[...] + nn(left[0:F, :], q_rows(sf_ref[dp * 8 + j]))


def apply(ig, tg, m, mo, sf, tt, pf):
    def whole(a):
        return pl.BlockSpec(a.shape, lambda j: (0,) * a.ndim)

    return pl.pallas_call(
        apply_kernel,
        grid=(8,),
        out_shape=(
            jax.ShapeDtypeStruct((TOK, 128), BF),
            jax.ShapeDtypeStruct((F, D), BF),
            jax.ShapeDtypeStruct((F, D), BF),
            jax.ShapeDtypeStruct((F, KC), F32),
        ),
        in_specs=[
            whole(ig),
            pl.BlockSpec((1, 4, F, 128), lambda j: (j // 2, j % 2, 0, 0)),
            pl.BlockSpec((1, F, 512), lambda j: (j // 2, 0, j % 2)),
            pl.BlockSpec((F, 128), lambda j: (0, j)),
            whole(sf), whole(tt), whole(pf),
        ],
        out_specs=[
            pl.BlockSpec((TOK, 128), lambda j: (0, 0)),
            pl.BlockSpec((F, 512), lambda j: (0, j)),
            pl.BlockSpec((F, 512), lambda j: (0, j)),
            pl.BlockSpec((F, 128), lambda j: (0, j)),
        ],
        scratch_shapes=[pltpu.VMEM((FP, 128), BF)],
        name="apply",
    )(ig, tg, m, mo, sf, tt, pf)


def body(inputs, out_grads, w_gate, w_up, w_down, err_down, mom_down, q_down):
    ig, tg, m, sf, tt, pf = exchange(
        inputs, out_grads, w_gate.T, w_up.T, w_down, err_down[0], mom_down, q_down.T
    )
    ig, nd, ne, nm = apply(ig, tg, m, mom_down, sf, tt, pf)
    return ig, nd, ne[None], nm


def solution(mesh):
    in_specs = (
        P("dp", None), P("dp", None), P(None, "mp"), P(None, "mp"), P("mp", None),
        P("dp", "mp", None), P("mp", "dp"), P(),
    )
    out_specs = (P("dp", "mp"), P("mp", None), P("dp", "mp", None), P("mp", "dp"))
    return jax.shard_map(body, mesh=mesh, in_specs=in_specs, out_specs=out_specs, check_vma=False)
```

```python
import jax
import jax.numpy as jnp
from jax import lax
from jax.experimental import pallas as pl
from jax.experimental.pallas import tpu as pltpu
from jax.sharding import PartitionSpec as P

MESH = pl.DeviceIdType.MESH
BF = jnp.bfloat16
F32 = jnp.float32
TOK, D, F, FP, R = 512, 4096, 344, 384, 8
UP = 352
KP = 768
KC = 1024
NK = D // KC
N_SEM = 112


def nt(a, b):
    return lax.dot_general(a, b, (((1,), (1,)), ((), ())), preferred_element_type=F32)


def nn(a, b):
    return lax.dot_general(a, b, (((1,), (0,)), ((), ())), preferred_element_type=F32)


def parts(v):
    hi = v.astype(BF).astype(F32)
    rest = v - hi
    mid = rest.astype(BF).astype(F32)
    return hi, mid, rest - mid


def split3(v):
    hi, mid, low = parts(v)
    return jnp.concatenate([hi, mid, low, jnp.zeros_like(v)], axis=0).astype(BF)


def fold(r):
    return (r[0:8] + r[8:16]) + r[16:24]


def wrap(v):
    return lax.rem(v, 4)


def step_kernel(
    x_h, dy_h, wg_h, wu_h, wd_h, er_h, mo_h, q_h,
    igs, tg, ms, mos, left, right,
    xs, dys, ws, wds, ers, qs, wsp,
    gu, dhq, ht, dt, dc, dcp, erq,
    pown, py_r, p3, pf, pg, ct, tt,
    sb, sc_r, sx_r, s1, sz_r, s2, sy_r, sf,
    rsf, rsp, hap, ham, hbp, hbm, rap, ram, rbp, rbm, a1, b1, za_r, xb_r,
    load_sem, send_sem, recv_sem,
):
    dp = lax.axis_index("dp")
    mp = lax.axis_index("mp")
    core = lax.rem(mp, 2)
    z = lax.rem(mp // 2, 4)
    x = mp // 8
    other = 1 - core
    to_core = (dp, mp + 1 - 2 * core)

    def to_x(d):
        return (dp, wrap(x + d) * 8 + z * 2 + core)

    def to_z(d):
        return (dp, x * 8 + wrap(z + d) * 2 + core)

    def to_y(d):
        return (wrap(dp + d), mp)

    barrier = pltpu.get_barrier_semaphore()
    peers = [to_core] + [f(d) for f in (to_x, to_z, to_y) for d in (1, 2, 3)]
    for peer in peers:
        pl.semaphore_signal(barrier, inc=1, device_id=peer, device_id_type=MESH)

    def lx(k):
        cols = pl.ds(k * 512, 512)
        return pltpu.make_async_copy(x_h.at[:, cols], xs.at[k], load_sem.at[k])

    def lwg(b):
        return pltpu.make_async_copy(
            wg_h.at[:, pl.ds(b * 128, 128)], ws.at[b // 2, b % 2, pl.ds(0, F)], load_sem.at[8 + b]
        )

    def lwu(b):
        return pltpu.make_async_copy(
            wu_h.at[:, pl.ds(b * 128, 128)], ws.at[b // 2, b % 2, pl.ds(UP, F)], load_sem.at[40 + b]
        )

    def ly(k):
        return pltpu.make_async_copy(dy_h.at[:, pl.ds(k * KC, KC)], dys.at[k], load_sem.at[72 + k])

    def lwd(k):
        return pltpu.make_async_copy(
            wd_h.at[:, pl.ds(k * KC, KC)], wds.at[k, pl.ds(0, F)], load_sem.at[76 + k]
        )

    def ler(k):
        return pltpu.make_async_copy(er_h.at[:, pl.ds(k * KC, KC)], ers.at[k], load_sem.at[80 + k])

    lmo = pltpu.make_async_copy(mo_h, mos, load_sem.at[84])
    lq = pltpu.make_async_copy(q_h, qs, load_sem.at[85])
    for k in range(8):
        lx(k).start()
        for b in range(4):
            lwg(4 * k + b).start()
            lwu(4 * k + b).start()
        if k == 1:
            lmo.start()
            lwd(dp).start()
    lq.start()
    ly(dp).start()
    for i in range(1, NK):
        ly(wrap(dp + i)).start()
        lwd(wrap(dp + i)).start()
    for k in range(NK):
        ler(k).start()

    count = [0]
    sent = []

    def send(src, dst, device):
        i = count[0]
        count[0] += 1
        c = pltpu.make_async_remote_copy(
            src_ref=src, dst_ref=dst, send_sem=send_sem.at[i], recv_sem=recv_sem.at[i],
            device_id=device, device_id_type=MESH,
        )
        c.start()
        sent.append(c)
        return c

    for ref in (gu, dhq, erq, pown):
        ref[...] = jnp.zeros_like(ref)
    ws[:, :, F:UP, :] = jnp.zeros((16, 2, UP - F, 128), BF)
    ws[:, :, UP + F :, :] = jnp.zeros((16, 2, KP - UP - F, 128), BF)
    wds[:, F:UP, :] = jnp.zeros((NK, UP - F, KC), BF)
    dt[F:UP, :] = jnp.zeros((UP - F, TOK), dt.dtype)
    dt[UP + F :, :] = jnp.zeros((KP - UP - F, TOK), dt.dtype)

    def gate_up(k):
        lx(k).wait()
        for b in range(4):
            lwg(4 * k + b).wait()
            lwu(4 * k + b).wait()
        w = jnp.concatenate([ws[2 * k + b // 2, b % 2, 0:704] for b in range(4)], axis=1)
        gu[...] += nt(w, xs[k])

    pl.loop(0, 2)(gate_up)

    pl.semaphore_wait(barrier, len(peers))
    lmo.wait()
    lwd(dp).wait()
    for p in range(8):
        lanes = pl.ds(p * 128, 128)
        tg[dp, p] = (wds[dp, 0:F, lanes].astype(F32) - 0.1 * (0.9 * mos[:, lanes])).astype(BF)
    y_right, y_left = wrap(dp + 1), wrap(dp + 3)
    t_right, t_left, t_far = {}, {}, []

    def t_own(*pieces):
        for p in pieces:
            t_right[p] = send(tg.at[dp, p], tg.at[dp, p], to_y(1))
            t_left[p] = send(tg.at[dp, p], tg.at[dp, p], to_y(3))

    def t_on(*pieces):
        for p in pieces:
            if p % 2 == 0:
                t_right[p].wait_recv()
                t_far.append(send(tg.at[y_left, p], tg.at[y_left, p], to_y(1)))
            else:
                t_left[p].wait_recv()
                t_far.append(send(tg.at[y_right, p], tg.at[y_right, p], to_y(3)))

    t_own(0, 1, 2)

    pl.loop(2, 8)(gate_up)
    c_w = send(ws.at[:, other], wsp, to_core)

    lq.wait()
    for k in range(NK):
        wds[k, UP:FP, :] = split3(qs[:, k * KC : (k + 1) * KC])

    @pl.loop(0, NK)
    def _(i):
        k = wrap(dp + i)
        ly(k).wait()

        @pl.when(i > 0)
        def _():
            lwd(k).wait()

        dhq[...] += nt(wds[k], dys[k])

    @pl.loop(0, NK)
    def _(k):
        ler(k).wait()
        erq[0:F, 0:32] += nt(ers[k], wds[k, UP:FP, :])

    @pl.loop(0, 4)
    def _(i):
        lanes = pl.ds(pl.multiple_of(i * 128, 128), 128)
        gv, uv, dv = gu[0:F, lanes], gu[UP : UP + F, lanes], dhq[0:F, lanes]
        sig = jax.nn.sigmoid(gv)
        gs = gv * sig
        ht[:, lanes] = (gs * uv).astype(BF)
        dt[0:F, lanes] = (dv * uv * sig * (1.0 + gv * (1.0 - sig))).astype(dt.dtype)
        dt[UP : UP + F, lanes] = (dv * gs).astype(dt.dtype)

    own_p = fold(nt(split3(fold(dhq[UP:FP, :])), ht[...]))
    pown[:, 0:F] = own_p + fold(erq[...].T[0:32, 0:F])
    c_py = [send(pown, py_r.at[d - 1], to_y(d)) for d in (1, 3, 2)]

    t_on(0, 1, 2)
    t_own(3)
    dc[...] = dt[...].T.astype(BF)
    c_dc = send(dc, dcp, to_core)

    @pl.loop(0, 8)
    def _(i):
        a = 2 * i
        r = nn(dc[...], jnp.concatenate([ws[a, core], ws[a + 1, core]], axis=1))
        rsf[i // 2, 2 * lax.rem(i, 2)] = r[:, 0:128]
        rsf[i // 2, 2 * lax.rem(i, 2) + 1] = r[:, 128:256]

    for c in c_py:
        c.wait_recv()
    pf[...] = ((pown[...] + py_r[1]) + (py_r[0] + py_r[2])) * 0.25
    base = core * 48 + z * 12
    for c in range(3):
        pg[base + x * 3 + c] = pf[:, c * 128 : (c + 1) * 128]
    own = pl.ds(base + x * 3, 3)
    c_pgx = [send(pg.at[own], pg.at[own], to_x(d)) for d in (1, 3, 2)]
    p3[...] = split3(pf[...])
    hp3 = split3(fold(nn(p3[:, 0:F], ht[...])))

    def s_part(c):
        s = fold(nn(hp3, dys[c]) + nn(p3[:, 0:F], ers[c]))
        for j in range(8):
            sb[8 * c + j] = s[:, j * 128 : (j + 1) * 128]

    s_part(2 * other)
    s_part(2 * other + 1)
    c_sc = send(sb.at[pl.ds(16 * other, 16)], sc_r, to_core)
    s_part(2 * core)
    s_part(2 * core + 1)
    t_on(3)
    t_own(4)

    c_w.wait_recv()
    c_dc.wait_recv()

    def rs_peer(i):
        a = 2 * i
        r = nn(dcp[...], jnp.concatenate([wsp[a], wsp[a + 1]], axis=1))
        for n in range(2):
            at = (i // 2, 2 * lax.rem(i, 2) + n)
            v = rsf[at] + r[:, n * 128 : (n + 1) * 128]
            rsf[at] = v
            rsp[at] = v.astype(BF)

    pl.loop(0, 3)(rs_peer)
    c_sc.wait_recv()
    half = pl.ds(16 * core, 16)
    sb[half] = sb[half] + sc_r[...]
    c_sx = [
        send(sb.at[pl.ds(16 * core + 4 * wrap(x + d), 4)], sx_r.at[d - 1], to_x(d))
        for d in (1, 3, 2)
    ]
    t_on(4)
    t_own(5)
    pl.loop(3, 8)(rs_peer)
    for c in c_pgx:
        c.wait_recv()
    own = pl.ds(base, 12)
    c_pgz = [send(pg.at[own], pg.at[own], to_z(d)) for d in (1, 3, 2)]
    x1, x2, x3 = wrap(x + 1), wrap(x + 2), wrap(x + 3)
    z1, z2, z3 = wrap(z + 1), wrap(z + 2), wrap(z + 3)
    q0, q1, q2, q3 = (pl.ds(n * 128, 128) for n in range(4))
    top, bottom = pl.ds(0, 256), pl.ds(256, 256)
    c_h = [
        send(rsp.at[x2, :, q0], hap, to_x(1)),
        send(rsp.at[x2, :, q1], ham, to_x(3)),
        send(rsp.at[:, z2, q2], hbp, to_z(1)),
        send(rsp.at[:, z2, q3], hbm, to_z(3)),
    ]
    for c in c_sx:
        c.wait_recv()
    s1[...] = (sb[pl.ds(16 * core + 4 * x, 4)] + sx_r[0]) + (sx_r[1] + sx_r[2])
    c_sz = [send(s1.at[wrap(z + d)], sz_r.at[d - 1], to_z(d)) for d in (1, 3, 2)]
    t_on(5)
    t_own(6)

    def m_part(k):
        ms[k] = nn(ht[...], dys[k]) + ers[k].astype(F32)

    pl.loop(0, 2)(m_part)
    for c in c_h:
        c.wait_recv()
    rsp[x1, :, q0] = (rsf[x1, :, q0] + hap[...].astype(F32)).astype(BF)
    rsp[x3, :, q1] = (rsf[x3, :, q1] + ham[...].astype(F32)).astype(BF)
    rsp[:, z1, q2] = (rsf[:, z1, q2] + hbp[...].astype(F32)).astype(BF)
    rsp[:, z3, q3] = (rsf[:, z3, q3] + hbm[...].astype(F32)).astype(BF)
    c_r = {}

    def bulk(j):
        zj, xj = wrap(z + j), wrap(x + j)
        c_r[j] = [
            send(rsp.at[x1, zj, top], rap.at[j], to_x(1)),
            send(rsp.at[x3, zj, top], ram.at[j], to_x(3)),
            send(rsp.at[xj, z1, bottom], rbp.at[j], to_z(1)),
            send(rsp.at[xj, z3, bottom], rbm.at[j], to_z(3)),
        ]

    bulk(1)
    bulk(2)
    for c in c_sz:
        c.wait_recv()
    s2[...] = (s1[z] + sz_r[0]) + (sz_r[1] + sz_r[2])
    c_sy = [send(s2, sy_r.at[d - 1], to_y(d)) for d in (1, 3, 2)]
    t_on(6)
    t_own(7)
    for c in c_pgz:
        c.wait_recv()
    own = pl.ds(core * 48, 48)
    c_pgc = send(pg.at[own], pg.at[own], to_core)
    bulk(3)
    pl.loop(2, 4)(m_part)
    c_pgc.wait_recv()
    for i in range(12):
        ct[:, i] = jnp.transpose(pg[8 * i : 8 * i + 8], (1, 0, 2))
    lane = lax.broadcasted_iota(jnp.int32, (1, 128), 1)
    done_b, done_t = [], []

    def total(v):
        v = jnp.sum(v, axis=0)
        return jnp.sum(jnp.sum(v, axis=0, keepdims=True), axis=1, keepdims=True)

    for k in range(R):
        v = ct[k]
        t = jnp.where(lane == k, 1.0, 0.0)
        coeffs = [total(b * v) for b in done_b]
        for c, b, tb in zip(coeffs, done_b, done_t):
            v = v - c[None] * b
            t = t - c * tb
        scale = lax.rsqrt(total(v * v) + 1e-06)
        done_b.append(v * scale[None])
        done_t.append(t * scale)
        tt[k : k + 1, :] = done_t[-1]

    for c in c_sy:
        c.wait_recv()
    s = (s2[...] + sy_r[1]) + (sy_r[0] + sy_r[2])
    q = jnp.zeros((R, 128), F32)
    for i in range(R):
        q += tt[:, i : i + 1] * s[i : i + 1, :]
    mine = core * 16 + x * 4 + z
    sf[mine] = q * 0.25
    c_gz = [send(sf.at[mine], sf.at[mine], to_z(d)) for d in (1, 3, 2)]
    t_on(7)
    bulk(0)
    p = jnp.zeros((R, FP), F32)
    for i in range(R):
        p += tt[:, i : i + 1] * pf[i : i + 1, :]
    hi, mid, low = parts(p)
    rows = [hi, hi, mid, hi, low, mid] + [jnp.zeros_like(p)] * 10
    left[...] = jnp.concatenate(rows, axis=0).T.astype(BF)
    right[48:128, :] = jnp.zeros((80, D), BF)

    def right_part(b):
        hi, mid, low = parts(sf[b])
        r = jnp.concatenate([hi, mid, hi, low, hi, mid], axis=0).astype(BF)
        right[0:48, pl.ds(pl.multiple_of(b * 128, 128), 128)] = r

    for c in c_gz:
        c.wait_recv()
    own = pl.ds(core * 16 + x * 4, 4)
    c_gx = [send(sf.at[own], sf.at[own], to_x(d)) for d in (1, 3, 2)]

    c_za, c_xb = [], []
    for j in (1, 2, 3, 0):
        for c in c_r[j]:
            c.wait_recv()
        a = rsf[x, wrap(z + j), top] + (rap[j].astype(F32) + ram[j].astype(F32))
        b = rsf[wrap(x + j), z, bottom] + (rbp[j].astype(F32) + rbm[j].astype(F32))
        if j == 0:
            break
        a1[j] = a.astype(BF)
        b1[j] = b.astype(BF)
        c_za.append(send(a1.at[j], za_r.at[j - 1], to_z(j)))
        c_xb.append(send(b1.at[j], xb_r.at[j - 1], to_x(j)))
    for c in c_gx:
        c.wait_recv()
    own = pl.ds(core * 16, 16)
    c_gc = send(sf.at[own], sf.at[own], to_core)
    for i in range(16):
        right_part(core * 16 + i)
    for c in c_za:
        c.wait_recv()
    igs[0:256, :] = (
        (a + za_r[0].astype(F32)) + (za_r[1].astype(F32) + za_r[2].astype(F32))
    ).astype(BF)
    for c in c_xb:
        c.wait_recv()
    igs[256:512, :] = (
        (b + xb_r[0].astype(F32)) + (xb_r[1].astype(F32) + xb_r[2].astype(F32))
    ).astype(BF)
    c_gc.wait_recv()
    for i in range(16):
        right_part(other * 16 + i)
    for p in range(8):
        if p % 2 == 0:
            t_left[p].wait_recv()
        else:
            t_right[p].wait_recv()
    for c in t_far:
        c.wait_recv()
    for c in sent:
        c.wait_send()


def exchange(x, dy, wg, wu, wd, er, mo, q):
    v = pltpu.VMEM
    any_spec = pl.BlockSpec(memory_space=pl.ANY)
    vmem_spec = pl.BlockSpec(memory_space=pltpu.VMEM)
    scratch = [
        v((8, TOK, 512), BF), v((NK, TOK, KC), BF), v((16, 2, KP, 128), BF),
        v((NK, FP, KC), BF), v((NK, F, KC), BF), v((R, D), F32), v((16, KP, 128), BF),
        v((704, TOK), F32), v((FP, TOK), F32), v((F, TOK), BF), v((KP, TOK), F32),
        v((TOK, KP), BF), v((TOK, KP), BF), v((FP, 128), F32),
        v((R, FP), F32), v((3, R, FP), F32), v((32, FP), BF), v((R, FP), F32),
        v((96, 8, 128), F32), v((8, 12, 8, 128), F32), v((8, 128), F32),
        v((32, 8, 128), F32), v((16, 8, 128), F32), v((3, 4, 8, 128), F32),
        v((4, 8, 128), F32), v((3, 8, 128), F32), v((8, 128), F32), v((3, 8, 128), F32),
        v((32, 8, 128), F32),
        v((4, 4, TOK, 128), F32), v((4, 4, TOK, 128), BF),
        v((4, 128, 128), BF), v((4, 128, 128), BF), v((4, 128, 128), BF), v((4, 128, 128), BF),
        v((4, 256, 128), BF), v((4, 256, 128), BF), v((4, 256, 128), BF), v((4, 256, 128), BF),
        v((4, 256, 128), BF), v((4, 256, 128), BF), v((3, 256, 128), BF), v((3, 256, 128), BF),
        pltpu.SemaphoreType.DMA((88,)),
        pltpu.SemaphoreType.DMA((N_SEM,)),
        pltpu.SemaphoreType.DMA((N_SEM,)),
    ]
    out_shape = (
        v((TOK, 128), BF), v((4, 8, F, 128), BF), v((NK, F, KC), F32), v((F, KC), F32),
        v((FP, 128), BF), v((128, D), BF),
    )
    return pl.pallas_call(
        step_kernel,
        out_shape=out_shape,
        in_specs=[any_spec] * 8,
        out_specs=[vmem_spec] * 6,
        scratch_shapes=scratch,
        compiler_params=pltpu.CompilerParams(
            collective_id=0, has_side_effects=True, vmem_limit_bytes=48 * 1024 * 1024
        ),
        name="exchange",
    )(x, dy, wg, wu, wd, er, mo, q)


def apply_kernel(ig, t_ref, m_ref, mo_ref, left, right, ig_o, nd_o, ne_o, nm_o, nd, ne, nm, sem):
    dp = lax.axis_index("dp")
    out_ig = pltpu.make_async_copy(ig, ig_o, sem.at[0])
    out_ig.start()
    l = left[0:F, :]
    copies = [out_ig]
    for j in range(8):
        cols = slice(j * 512, (j + 1) * 512)
        approx = nn(l, right[:, cols])
        half = slice((j % 2) * 512, (j % 2) * 512 + 512)
        ne[:, cols] = (m_ref[j // 2, :, half] - approx).astype(BF)
        for c in range(4):
            lanes = slice(c * 128, (c + 1) * 128)
            b = 4 * j + c
            nd[:, b * 128 : (b + 1) * 128] = (
                t_ref[b // 8, b % 8].astype(F32) - 0.1 * approx[:, lanes]
            ).astype(BF)
        for n, (src, dst) in enumerate(((ne, ne_o), (nd, nd_o))):
            copies.append(
                pltpu.make_async_copy(
                    src.at[:, pl.ds(j * 512, 512)], dst.at[:, pl.ds(j * 512, 512)],
                    sem.at[1 + 2 * j + n],
                )
            )
            copies[-1].start()
        if j % 4 == 1:
            h = j // 4
            cols = pl.ds(pl.multiple_of(dp * KC + h * 512, 512), 512)
            nm[:, h * 512 : (h + 1) * 512] = 0.9 * mo_ref[:, h * 512 : (h + 1) * 512] + nn(
                l, right[:, cols]
            )
            copies.append(
                pltpu.make_async_copy(
                    nm.at[:, pl.ds(h * 512, 512)], nm_o.at[:, pl.ds(h * 512, 512)], sem.at[17 + h]
                )
            )
            copies[-1].start()
    for c in copies:
        c.wait()


def apply(*args):
    v = pltpu.VMEM
    args = [pltpu.with_memory_space_constraint(a, pltpu.VMEM) for a in args]
    return pl.pallas_call(
        apply_kernel,
        out_shape=(
            jax.ShapeDtypeStruct((TOK, 128), BF),
            jax.ShapeDtypeStruct((F, D), BF),
            jax.ShapeDtypeStruct((F, D), BF),
            jax.ShapeDtypeStruct((F, KC), F32),
        ),
        in_specs=[pl.BlockSpec(memory_space=pltpu.VMEM)] * len(args),
        out_specs=[pl.BlockSpec(memory_space=pl.ANY)] * 4,
        scratch_shapes=[
            v((F, D), BF), v((F, D), BF), v((F, KC), F32), pltpu.SemaphoreType.DMA((20,)),
        ],
        compiler_params=pltpu.CompilerParams(vmem_limit_bytes=24 * 1024 * 1024),
        name="apply",
    )(*args)


def body(inputs, out_grads, w_gate, w_up, w_down, err_down, mom_down, q_down):
    kept = exchange(
        inputs, out_grads, w_gate.T, w_up.T, w_down, err_down[0], mom_down, q_down.T
    )
    ig, nd, ne, nm = apply(*kept)
    return ig, nd, ne[None], nm


def solution(mesh):
    in_specs = (
        P("dp", None), P("dp", None), P(None, "mp"), P(None, "mp"), P("mp", None),
        P("dp", "mp", None), P("mp", "dp"), P(),
    )
    out_specs = (P("dp", "mp"), P("mp", None), P("dp", "mp", None), P("mp", "dp"))
    return jax.shard_map(body, mesh=mesh, in_specs=in_specs, out_specs=out_specs, check_vma=False)
```

```python
import jax
import jax.numpy as jnp
from jax import lax
from jax.experimental import pallas as pl
from jax.experimental.pallas import tpu as pltpu
from jax.sharding import PartitionSpec as P

MESH = pl.DeviceIdType.MESH
BF = jnp.bfloat16
F32 = jnp.float32
TOK, D, F, FP, R = 512, 4096, 344, 384, 8
UP = 352
KP = 768
KC = 1024
NK = D // KC
N_SEM = 32
PLANE = [(i, j) for i in range(4) for j in range(4) if i or j]


def nt(a, b):
    return lax.dot_general(a, b, (((1,), (1,)), ((), ())), preferred_element_type=F32)


def nn(a, b):
    return lax.dot_general(a, b, (((1,), (0,)), ((), ())), preferred_element_type=F32)


def parts(v):
    hi = v.astype(BF).astype(F32)
    rest = v - hi
    mid = rest.astype(BF).astype(F32)
    return hi, mid, rest - mid


def split3(v):
    hi, mid, low = parts(v)
    return jnp.concatenate([hi, mid, low, jnp.zeros_like(v)], axis=0).astype(BF)


def fold(r):
    return (r[0:8] + r[8:16]) + r[16:24]


def wrap(v):
    return lax.rem(v, 4)


def step_kernel(
    x_h, dy_h, wg_h, wu_h, wd_h, er_h, mo_h, q_h,
    igs, tg, ms, mos, left, right,
    xs, dys, ws, wds, ers, qs, wsp,
    gu, dhq, ht, dt, dc, dcp, erq,
    pown, py_r, p3, pf, pg, ct, tt,
    sb, sc_r, sp_r, s2, sy_r, sf,
    rsf, rsp, rr, a1, b1, zx,
    load_sem, send_sem, recv_sem,
):
    dp = lax.axis_index("dp")
    mp = lax.axis_index("mp")
    core = lax.rem(mp, 2)
    z = lax.rem(mp // 2, 4)
    x = mp // 8
    other = 1 - core
    to_core = (dp, mp + 1 - 2 * core)

    def to_x(d):
        return (dp, wrap(x + d) * 8 + z * 2 + core)

    def to_z(d):
        return (dp, x * 8 + wrap(z + d) * 2 + core)

    def to_y(d):
        return (wrap(dp + d), mp)

    def to_plane(i, j):
        return (dp, wrap(x + i) * 8 + wrap(z + j) * 2 + core)

    barrier = pltpu.get_barrier_semaphore()
    peers = [to_core] + [to_plane(i, j) for i, j in PLANE] + [to_y(d) for d in (1, 2, 3)]
    for peer in peers:
        pl.semaphore_signal(barrier, inc=1, device_id=peer, device_id_type=MESH)

    def lx(k):
        cols = pl.ds(k * 512, 512)
        return pltpu.make_async_copy(x_h.at[:, cols], xs.at[k], load_sem.at[k])

    def lwg(k):
        cols = pl.ds(k * 512, 512)
        return pltpu.make_async_copy(wg_h.at[:, cols], ws.at[k, pl.ds(0, F)], load_sem.at[8 + k])

    def lwu(k):
        cols = pl.ds(k * 512, 512)
        return pltpu.make_async_copy(wu_h.at[:, cols], ws.at[k, pl.ds(UP, F)], load_sem.at[16 + k])

    def ly(k):
        return pltpu.make_async_copy(dy_h.at[:, pl.ds(k * KC, KC)], dys.at[k], load_sem.at[24 + k])

    def lwd(k):
        return pltpu.make_async_copy(
            wd_h.at[:, pl.ds(k * KC, KC)], wds.at[k, pl.ds(0, F)], load_sem.at[28 + k]
        )

    def ler(k):
        return pltpu.make_async_copy(er_h.at[:, pl.ds(k * KC, KC)], ers.at[k], load_sem.at[32])

    lmo = pltpu.make_async_copy(mo_h, mos, load_sem.at[33])
    lq = pltpu.make_async_copy(q_h, qs, load_sem.at[34])
    for k in range(8):
        lx(k).start()
        lwg(k).start()
        lwu(k).start()
        if k == 1:
            lmo.start()
            lwd(dp).start()
    lq.start()
    ly(dp).start()
    for i in range(1, NK):
        ly(wrap(dp + i)).start()
        lwd(wrap(dp + i)).start()
    for k in range(NK):
        ler(k).start()

    count = [0]
    sent = []

    class Exchange:
        def __init__(self, whole):
            i = count[0]
            count[0] += 1
            self.sems = send_sem.at[i], recv_sem.at[i]
            self.whole = whole
            sent.append(self)

        def send(self, src, dst, device):
            pltpu.make_async_remote_copy(
                src_ref=src, dst_ref=dst, send_sem=self.sems[0], recv_sem=self.sems[1],
                device_id=device, device_id_type=MESH,
            ).start()
            return self

        def wait_send(self):
            pltpu.make_async_copy(self.whole, self.whole, self.sems[0]).wait()

        def wait_recv(self):
            pltpu.make_async_copy(self.whole, self.whole, self.sems[1]).wait()

    def send(src, dst, device):
        return Exchange(dst).send(src, dst, device)

    for ref in (gu, dhq, erq, pown):
        ref[...] = jnp.zeros_like(ref)
    ws[:, F:UP, :] = jnp.zeros((8, UP - F, 512), BF)
    ws[:, UP + F :, :] = jnp.zeros((8, KP - UP - F, 512), BF)
    wds[:, F:UP, :] = jnp.zeros((NK, UP - F, KC), BF)
    dt[F:UP, :] = jnp.zeros((UP - F, TOK), dt.dtype)
    dt[UP + F :, :] = jnp.zeros((KP - UP - F, TOK), dt.dtype)

    def arrived(k):
        lx(k).wait()
        lwg(k).wait()
        lwu(k).wait()

    @pl.loop(0, 2)
    def _(k):
        arrived(k)
        gu[...] += nt(ws[k, 0:704], xs[k])

    pl.semaphore_wait(barrier, len(peers))
    lmo.wait()
    lwd(dp).wait()
    for p in range(8):
        lanes = pl.ds(p * 128, 128)
        tg[dp, p] = (wds[dp, 0:F, lanes].astype(F32) - 0.1 * (0.9 * mos[:, lanes])).astype(BF)
    y_right, y_left = wrap(dp + 1), wrap(dp + 3)

    def t_own(lo, n):
        at = tg.at[dp, pl.ds(lo, n)]
        return send(at, at, to_y(1)), send(at, at, to_y(3))

    def t_right(lo, n):
        at = tg.at[y_left, pl.ds(lo, n)]
        return send(at, at, to_y(1))

    def t_left(lo, n):
        at = tg.at[y_right, pl.ds(lo, n)]
        return send(at, at, to_y(3))

    t0 = t_own(0, 4)

    @pl.loop(1, 4)
    def _(k):
        arrived(2 * k)
        arrived(2 * k + 1)
        w = jnp.concatenate([ws[2 * k, 0:704], ws[2 * k + 1, 0:704]], axis=1)
        gu[...] += nt(w, jnp.concatenate([xs[2 * k], xs[2 * k + 1]], axis=1))

    def half_lanes(c, n):
        return pl.ds(pl.multiple_of(c * 128 + n * 256, 128), 128)

    c_w = Exchange(wsp)
    for n in range(2):
        c_w.send(ws.at[:, :, half_lanes(other, n)], wsp.at[:, :, pl.ds(n * 128, 128)], to_core)

    lq.wait()
    for k in range(NK):
        wds[k, UP:FP, :] = split3(qs[:, k * KC : (k + 1) * KC])

    @pl.loop(0, NK)
    def _(i):
        k = wrap(dp + i)
        ly(k).wait()

        @pl.when(i > 0)
        def _():
            lwd(k).wait()

        dhq[...] += nt(wds[k], dys[k])

    pltpu.make_async_copy(er_h, er_h, load_sem.at[32]).wait()

    @pl.loop(0, NK)
    def _(k):
        erq[0:F, 0:32] += nt(ers[k], wds[k, UP:FP, :])

    @pl.loop(0, 4)
    def _(i):
        lanes = pl.ds(pl.multiple_of(i * 128, 128), 128)
        gv, uv, dv = gu[0:F, lanes], gu[UP : UP + F, lanes], dhq[0:F, lanes]
        sig = jax.nn.sigmoid(gv)
        gs = gv * sig
        ht[:, lanes] = (gs * uv).astype(BF)
        dt[0:F, lanes] = (dv * uv * sig * (1.0 + gv * (1.0 - sig))).astype(dt.dtype)
        dt[UP : UP + F, lanes] = (dv * gs).astype(dt.dtype)

    own_p = fold(nt(split3(fold(dhq[UP:FP, :])), ht[...]))
    pown[:, 0:F] = own_p + fold(erq[...].T[0:32, 0:F])
    c_py = Exchange(py_r)
    for d in (1, 3, 2):
        c_py.send(pown, py_r.at[d - 1], to_y(d))
    t1 = t_own(4, 2)

    dc[...] = dt[...].T.astype(BF)
    c_dc = send(dc, dcp, to_core)

    @pl.loop(0, 4)
    def _(i):
        w = [ws[2 * i + n // 2, :, half_lanes(core, n % 2)] for n in range(4)]
        r = nn(dc[...], jnp.concatenate(w, axis=1))
        for n in range(4):
            rsf[i, n] = r[:, n * 128 : (n + 1) * 128]

    t0[0].wait_recv()
    t0[1].wait_recv()
    far = [t_right(0, 2), t_left(2, 2)]
    t2 = t_own(6, 1)
    c_py.wait_recv()
    pf[...] = ((pown[...] + py_r[1]) + (py_r[0] + py_r[2])) * 0.25
    base = core * 48 + z * 12
    for c in range(3):
        pg[base + x * 3 + c] = pf[:, c * 128 : (c + 1) * 128]
    own = pl.ds(base + x * 3, 3)
    c_pg = Exchange(pg.at[pl.ds(0, 45)])
    for i, j in PLANE:
        c_pg.send(pg.at[own], pg.at[own], to_plane(i, j))
    p3[...] = split3(pf[...])
    hp3 = split3(fold(nn(p3[:, 0:F], ht[...])))

    def s_part(c):
        s = fold(nn(hp3, dys[c]) + nn(p3[:, 0:F], ers[c]))
        for j in range(8):
            sb[8 * c + j] = s[:, j * 128 : (j + 1) * 128]

    s_part(2 * other)
    s_part(2 * other + 1)
    c_sc = send(sb.at[pl.ds(16 * other, 16)], sc_r, to_core)
    s_part(2 * core)
    s_part(2 * core + 1)

    c_w.wait_recv()
    c_dc.wait_recv()

    def rs_peer(i):
        r = nn(dcp[...], jnp.concatenate([wsp[2 * i], wsp[2 * i + 1]], axis=1))
        for n in range(4):
            v = rsf[i, n] + r[:, n * 128 : (n + 1) * 128]
            rsf[i, n] = v
            rsp[i, n] = v.astype(BF)

    pl.loop(0, 2)(rs_peer)
    c_sc.wait_recv()
    half = pl.ds(16 * core, 16)
    sb[half] = sb[half] + sc_r[...]
    c_sp = Exchange(sp_r)
    for i, j in PLANE:
        c_sp.send(
            sb.at[16 * core + 4 * wrap(x + i) + wrap(z + j)], sp_r.at[4 * i + j - 1], to_plane(i, j)
        )
    pl.loop(2, 4)(rs_peer)
    top, bottom = pl.ds(0, 256), pl.ds(256, 256)
    c_r = {}

    def bulk(j):
        zj, xj = wrap(z + j), wrap(x + j)
        c_r[j] = Exchange(rr.at[j])
        for d in (1, 3, 2):
            c_r[j].send(rsp.at[wrap(x + d), zj, top], rr.at[j, d - 1], to_x(d))
            c_r[j].send(rsp.at[xj, wrap(z + d), bottom], rr.at[j, d + 2], to_z(d))

    bulk(1)
    bulk(2)
    c_pg.wait_recv()
    own = pl.ds(core * 48, 48)
    c_pgc = send(pg.at[own], pg.at[own], to_core)
    c_sp.wait_recv()
    mine = core * 16 + x * 4 + z
    s2[...] = jnp.sum(sp_r[...], axis=0) + sb[mine]
    c_sy = Exchange(sy_r)
    for d in (1, 3, 2):
        c_sy.send(s2, sy_r.at[d - 1], to_y(d))
    t3 = t_own(7, 1)
    t1[0].wait_recv()
    far.append(t_right(4, 1))
    t1[1].wait_recv()
    far.append(t_left(5, 1))

    c_pgc.wait_recv()
    for i in range(12):
        ct[:, i] = jnp.transpose(pg[8 * i : 8 * i + 8], (1, 0, 2))
    lane = lax.broadcasted_iota(jnp.int32, (1, 128), 1)
    done_b, done_t = [], []

    def total(v):
        v = jnp.sum(v, axis=0)
        return jnp.sum(jnp.sum(v, axis=0, keepdims=True), axis=1, keepdims=True)

    for k in range(R):
        v = ct[k]
        t = jnp.where(lane == k, 1.0, 0.0)
        coeffs = [total(b * v) for b in done_b]
        for c, b, tb in zip(coeffs, done_b, done_t):
            v = v - c[None] * b
            t = t - c * tb
        scale = lax.rsqrt(total(v * v) + 1e-06)
        done_b.append(v * scale[None])
        done_t.append(t * scale)
        tt[k : k + 1, :] = done_t[-1]

    c_sy.wait_recv()
    s = (s2[...] + sy_r[1]) + (sy_r[0] + sy_r[2])
    q = jnp.zeros((R, 128), F32)
    for i in range(R):
        q += tt[:, i : i + 1] * s[i : i + 1, :]
    sf[mine] = q * 0.25
    c_g = Exchange(sf.at[pl.ds(0, 15)])
    for i, j in PLANE:
        c_g.send(sf.at[mine], sf.at[mine], to_plane(i, j))
    bulk(3)
    bulk(0)
    t2[0].wait_recv()
    far.append(t_right(6, 1))

    @pl.loop(0, NK)
    def _(k):
        ms[k] = nn(ht[...], dys[k]) + ers[k].astype(F32)

    c_zx = Exchange(zx)

    def first_sums(j):
        c_r[j].wait_recv()
        a = rsf[x, wrap(z + j), top]
        b = rsf[wrap(x + j), z, bottom]
        for d in range(3):
            a += rr[j, d].astype(F32)
            b += rr[j, d + 3].astype(F32)
        return a, b

    def second(j):
        a, b = first_sums(j)
        a1[j] = a.astype(BF)
        b1[j] = b.astype(BF)
        c_zx.send(a1.at[j], zx.at[j - 1], to_z(j))
        c_zx.send(b1.at[j], zx.at[j + 2], to_x(j))

    second(1)
    second(2)
    t3[1].wait_recv()
    far.append(t_left(7, 1))

    p = jnp.zeros((R, FP), F32)
    for i in range(R):
        p += tt[:, i : i + 1] * pf[i : i + 1, :]
    hi, mid, low = parts(p)
    rows = [hi, hi, mid, hi, low, mid] + [jnp.zeros_like(p)] * 10
    left[...] = jnp.concatenate(rows, axis=0).T.astype(BF)
    right[48:128, :] = jnp.zeros((80, D), BF)

    def right_part(b):
        hi, mid, low = parts(sf[b])
        r = jnp.concatenate([hi, mid, hi, low, hi, mid], axis=0).astype(BF)
        right[0:48, pl.ds(pl.multiple_of(b * 128, 128), 128)] = r

    c_g.wait_recv()
    own = pl.ds(core * 16, 16)
    c_gc = send(sf.at[own], sf.at[own], to_core)
    for i in range(16):
        right_part(core * 16 + i)
    second(3)
    a, b = first_sums(0)
    c_gc.wait_recv()
    for i in range(16):
        right_part(other * 16 + i)
    c_zx.wait_recv()
    for d in range(3):
        a += zx[d].astype(F32)
        b += zx[d + 3].astype(F32)
    igs[0:256, :] = a.astype(BF)
    igs[256:512, :] = b.astype(BF)
    for c in (t2[1], t3[0], *far):
        c.wait_recv()
    for c in sent:
        c.wait_send()


def exchange(x, dy, wg, wu, wd, er, mo, q):
    v = pltpu.VMEM
    any_spec = pl.BlockSpec(memory_space=pl.ANY)
    vmem_spec = pl.BlockSpec(memory_space=pltpu.VMEM)
    scratch = [
        v((8, TOK, 512), BF), v((NK, TOK, KC), BF), v((8, KP, 512), BF),
        v((NK, FP, KC), BF), v((NK, F, KC), BF), v((R, D), F32), v((8, KP, 256), BF),
        v((704, TOK), F32), v((FP, TOK), F32), v((F, TOK), BF), v((KP, TOK), F32),
        v((TOK, KP), BF), v((TOK, KP), BF), v((FP, 128), F32),
        v((R, FP), F32), v((3, R, FP), F32), v((32, FP), BF), v((R, FP), F32),
        v((96, 8, 128), F32), v((8, 12, 8, 128), F32), v((8, 128), F32),
        v((32, 8, 128), F32), v((16, 8, 128), F32), v((15, 8, 128), F32),
        v((8, 128), F32), v((3, 8, 128), F32), v((32, 8, 128), F32),
        v((4, 4, TOK, 128), F32), v((4, 4, TOK, 128), BF), v((4, 6, 256, 128), BF),
        v((4, 256, 128), BF), v((4, 256, 128), BF), v((6, 256, 128), BF),
        pltpu.SemaphoreType.DMA((35,)),
        pltpu.SemaphoreType.DMA((N_SEM,)),
        pltpu.SemaphoreType.DMA((N_SEM,)),
    ]
    out_shape = (
        v((TOK, 128), BF), v((4, 8, F, 128), BF), v((NK, F, KC), F32), v((F, KC), F32),
        v((FP, 128), BF), v((128, D), BF),
    )
    return pl.pallas_call(
        step_kernel,
        out_shape=out_shape,
        in_specs=[any_spec] * 8,
        out_specs=[vmem_spec] * 6,
        scratch_shapes=scratch,
        compiler_params=pltpu.CompilerParams(
            collective_id=0, has_side_effects=True, vmem_limit_bytes=48 * 1024 * 1024
        ),
        name="exchange",
    )(x, dy, wg, wu, wd, er, mo, q)


def apply_kernel(ig, t_ref, m_ref, mo_ref, left, right, ig_o, nd_o, ne_o, nm_o, nd, ne, nm, sem):
    dp = lax.axis_index("dp")
    out_ig = pltpu.make_async_copy(ig, ig_o, sem.at[0])
    out_ig.start()
    l = left[0:F, :]
    copies = [out_ig]
    for j in range(8):
        cols = slice(j * 512, (j + 1) * 512)
        approx = nn(l, right[:, cols])
        half = slice((j % 2) * 512, (j % 2) * 512 + 512)
        ne[:, cols] = (m_ref[j // 2, :, half] - approx).astype(BF)
        for c in range(4):
            lanes = slice(c * 128, (c + 1) * 128)
            b = 4 * j + c
            nd[:, b * 128 : (b + 1) * 128] = (
                t_ref[b // 8, b % 8].astype(F32) - 0.1 * approx[:, lanes]
            ).astype(BF)
        for n, (src, dst) in enumerate(((ne, ne_o), (nd, nd_o))):
            copies.append(
                pltpu.make_async_copy(
                    src.at[:, pl.ds(j * 512, 512)], dst.at[:, pl.ds(j * 512, 512)],
                    sem.at[1 + 2 * j + n],
                )
            )
            copies[-1].start()
        if j % 4 == 1:
            h = j // 4
            cols = pl.ds(pl.multiple_of(dp * KC + h * 512, 512), 512)
            nm[:, h * 512 : (h + 1) * 512] = 0.9 * mo_ref[:, h * 512 : (h + 1) * 512] + nn(
                l, right[:, cols]
            )
            copies.append(
                pltpu.make_async_copy(
                    nm.at[:, pl.ds(h * 512, 512)], nm_o.at[:, pl.ds(h * 512, 512)], sem.at[17 + h]
                )
            )
            copies[-1].start()
    for c in copies:
        c.wait()


def apply(*args):
    v = pltpu.VMEM
    args = [pltpu.with_memory_space_constraint(a, pltpu.VMEM) for a in args]
    return pl.pallas_call(
        apply_kernel,
        out_shape=(
            jax.ShapeDtypeStruct((TOK, 128), BF),
            jax.ShapeDtypeStruct((F, D), BF),
            jax.ShapeDtypeStruct((F, D), BF),
            jax.ShapeDtypeStruct((F, KC), F32),
        ),
        in_specs=[pl.BlockSpec(memory_space=pltpu.VMEM)] * len(args),
        out_specs=[pl.BlockSpec(memory_space=pl.ANY)] * 4,
        scratch_shapes=[
            v((F, D), BF), v((F, D), BF), v((F, KC), F32), pltpu.SemaphoreType.DMA((20,)),
        ],
        compiler_params=pltpu.CompilerParams(vmem_limit_bytes=24 * 1024 * 1024),
        name="apply",
    )(*args)


def body(inputs, out_grads, w_gate, w_up, w_down, err_down, mom_down, q_down):
    kept = exchange(
        inputs, out_grads, w_gate.T, w_up.T, w_down, err_down[0], mom_down, q_down.T
    )
    ig, nd, ne, nm = apply(*kept)
    return ig, nd, ne[None], nm


def solution(mesh):
    in_specs = (
        P("dp", None), P("dp", None), P(None, "mp"), P(None, "mp"), P("mp", None),
        P("dp", "mp", None), P("mp", "dp"), P(),
    )
    out_specs = (P("dp", "mp"), P("mp", None), P("dp", "mp", None), P("mp", "dp"))
    return jax.shard_map(body, mesh=mesh, in_specs=in_specs, out_specs=out_specs, check_vma=False)
```

```python
import jax
import jax.numpy as jnp
from jax import lax
from jax.experimental import pallas as pl
from jax.experimental.pallas import tpu as pltpu
from jax.sharding import PartitionSpec as P

MESH = pl.DeviceIdType.MESH
BF = jnp.bfloat16
F32 = jnp.float32
TOK, D, F, FP, R = 512, 4096, 344, 384, 8
UP = 352
KP = 768
KC = 1024
NK = D // KC
N_SEM = 34
PLANE = [(i, j) for i in range(4) for j in range(4) if i or j]


def nt(a, b):
    return lax.dot_general(a, b, (((1,), (1,)), ((), ())), preferred_element_type=F32)


def nn(a, b):
    return lax.dot_general(a, b, (((1,), (0,)), ((), ())), preferred_element_type=F32)


def parts(v):
    hi = v.astype(BF).astype(F32)
    rest = v - hi
    mid = rest.astype(BF).astype(F32)
    return hi, mid, rest - mid


def split3(v):
    hi, mid, low = parts(v)
    return jnp.concatenate([hi, mid, low, jnp.zeros_like(v)], axis=0).astype(BF)


def fold(r):
    return (r[0:8] + r[8:16]) + r[16:24]


def wrap(v):
    return lax.rem(v, 4)


def step_kernel(
    x_h, dy_h, wg_h, wu_h, wd_h, er_h, mo_h, q_h,
    igs, ne, tg, ms, mos, left, right,
    xs, dys, ws, wds, ers, qs, wsp,
    gu, dhq, ht, dt, dc, dcp, erq,
    pown, py_r, p3, pf, pg, ct, tt,
    sb, sc_r, sp_r, s2, sy_r, sf,
    rsf, rsp, ha, hb, ra, rb, a1, b1, zx,
    load_sem, send_sem, recv_sem,
):
    dp = lax.axis_index("dp")
    mp = lax.axis_index("mp")
    core = lax.rem(mp, 2)
    z = lax.rem(mp // 2, 4)
    x = mp // 8
    other = 1 - core
    to_core = (dp, mp + 1 - 2 * core)

    def to_x(d):
        return (dp, wrap(x + d) * 8 + z * 2 + core)

    def to_z(d):
        return (dp, x * 8 + wrap(z + d) * 2 + core)

    def to_y(d):
        return (wrap(dp + d), mp)

    def to_plane(i, j):
        return (dp, wrap(x + i) * 8 + wrap(z + j) * 2 + core)

    barrier = pltpu.get_barrier_semaphore()
    peers = [to_core] + [to_plane(i, j) for i, j in PLANE] + [to_y(d) for d in (1, 2, 3)]
    for peer in peers:
        pl.semaphore_signal(barrier, inc=1, device_id=peer, device_id_type=MESH)

    def group(k):
        return k if k < 2 else 1 + k // 2

    def lx(k):
        cols = pl.ds(k * 512, 512)
        return pltpu.make_async_copy(x_h.at[:, cols], xs.at[k], load_sem.at[group(k)])

    def lwg(k):
        cols = pl.ds(k * 512, 512)
        return pltpu.make_async_copy(wg_h.at[:, cols], ws.at[k, pl.ds(0, F)], load_sem.at[5 + group(k)])

    def lwu(k):
        cols = pl.ds(k * 512, 512)
        return pltpu.make_async_copy(wu_h.at[:, cols], ws.at[k, pl.ds(UP, F)], load_sem.at[5 + group(k)])

    def arrived(k, n, sem):
        at = xs.at[pl.ds(k, n)]
        pltpu.make_async_copy(at, at, load_sem.at[sem]).wait()
        at = ws.at[pl.ds(k, n), pl.ds(0, 2 * F)]
        pltpu.make_async_copy(at, at, load_sem.at[5 + sem]).wait()

    def ly(k):
        return pltpu.make_async_copy(dy_h.at[:, pl.ds(k * KC, KC)], dys.at[k], load_sem.at[10 + k])

    def lwd(k):
        return pltpu.make_async_copy(
            wd_h.at[:, pl.ds(k * KC, KC)], wds.at[k, pl.ds(0, F)], load_sem.at[14 + k]
        )

    def ler(k):
        return pltpu.make_async_copy(er_h.at[:, pl.ds(k * KC, KC)], ers.at[k], load_sem.at[18])

    lmo = pltpu.make_async_copy(mo_h, mos, load_sem.at[19])
    lq = pltpu.make_async_copy(q_h, qs, load_sem.at[20])
    for k in range(8):
        lx(k).start()
        lwg(k).start()
        lwu(k).start()
        if k == 3:
            lmo.start()
            lwd(dp).start()
    lq.start()
    ly(dp).start()
    for i in range(1, NK):
        ly(wrap(dp + i)).start()
        lwd(wrap(dp + i)).start()
    for k in range(NK):
        ler(k).start()

    count = [0]
    sent = []

    class Exchange:
        def __init__(self, whole):
            i = count[0]
            count[0] += 1
            self.sems = send_sem.at[i], recv_sem.at[i]
            self.whole = whole
            sent.append(self)

        def send(self, src, dst, device):
            pltpu.make_async_remote_copy(
                src_ref=src, dst_ref=dst, send_sem=self.sems[0], recv_sem=self.sems[1],
                device_id=device, device_id_type=MESH,
            ).start()
            return self

        def wait_send(self):
            pltpu.make_async_copy(self.whole, self.whole, self.sems[0]).wait()

        def wait_recv(self):
            pltpu.make_async_copy(self.whole, self.whole, self.sems[1]).wait()

    def send(src, dst, device):
        return Exchange(dst).send(src, dst, device)

    for ref in (gu, dhq, erq, pown):
        ref[...] = jnp.zeros_like(ref)
    ws[:, F:UP, :] = jnp.zeros((8, UP - F, 512), BF)
    ws[:, UP + F :, :] = jnp.zeros((8, KP - UP - F, 512), BF)
    wds[:, F:UP, :] = jnp.zeros((NK, UP - F, KC), BF)
    dt[F:UP, :] = jnp.zeros((UP - F, TOK), dt.dtype)
    dt[UP + F :, :] = jnp.zeros((KP - UP - F, TOK), dt.dtype)

    @pl.loop(0, 2)
    def _(k):
        arrived(k, 1, k)
        gu[...] += nt(ws[k, 0:704], xs[k])

    def gate_up(k):
        arrived(2 * k, 2, 1 + k)
        w = jnp.concatenate([ws[2 * k, 0:704], ws[2 * k + 1, 0:704]], axis=1)
        gu[...] += nt(w, jnp.concatenate([xs[2 * k], xs[2 * k + 1]], axis=1))

    pl.loop(1, 2)(gate_up)
    pl.semaphore_wait(barrier, len(peers))
    lmo.wait()
    lwd(dp).wait()
    for p in range(8):
        lanes = pl.ds(p * 128, 128)
        tg[dp, p] = (wds[dp, 0:F, lanes].astype(F32) - 0.1 * (0.9 * mos[:, lanes])).astype(BF)
    y_right, y_left = wrap(dp + 1), wrap(dp + 3)

    def t_own(lo, n):
        at = tg.at[dp, pl.ds(lo, n)]
        return send(at, at, to_y(1)), send(at, at, to_y(3))

    def t_right(lo, n):
        at = tg.at[y_left, pl.ds(lo, n)]
        return send(at, at, to_y(1))

    def t_left(lo, n):
        at = tg.at[y_right, pl.ds(lo, n)]
        return send(at, at, to_y(3))

    t0 = t_own(0, 3)

    pl.loop(2, 4)(gate_up)

    def half_lanes(c, n):
        return pl.ds(pl.multiple_of(c * 128 + n * 256, 128), 128)

    c_w = Exchange(wsp)
    for n in range(2):
        c_w.send(ws.at[:, :, half_lanes(other, n)], wsp.at[:, :, pl.ds(n * 128, 128)], to_core)

    lq.wait()
    for k in range(NK):
        wds[k, UP:FP, :] = split3(qs[:, k * KC : (k + 1) * KC])

    @pl.loop(0, 2)
    def _(i):
        k, n = wrap(dp + 2 * i), wrap(dp + 2 * i + 1)
        ly(k).wait()
        ly(n).wait()
        lwd(n).wait()

        @pl.when(i > 0)
        def _():
            lwd(k).wait()

        dhq[...] += nt(
            jnp.concatenate([wds[k], wds[n]], axis=1), jnp.concatenate([dys[k], dys[n]], axis=1)
        )

    pltpu.make_async_copy(er_h, er_h, load_sem.at[18]).wait()
    erq[0:F, 0:32] = nt(
        jnp.concatenate([ers[k] for k in range(NK)], axis=1),
        jnp.concatenate([wds[k, UP:FP, :] for k in range(NK)], axis=1),
    )

    @pl.loop(0, 4)
    def _(i):
        lanes = pl.ds(pl.multiple_of(i * 128, 128), 128)
        gv, uv, dv = gu[0:F, lanes], gu[UP : UP + F, lanes], dhq[0:F, lanes]
        sig = jax.nn.sigmoid(gv)
        gs = gv * sig
        ht[:, lanes] = (gs * uv).astype(BF)
        dt[0:F, lanes] = (dv * uv * sig * (1.0 + gv * (1.0 - sig))).astype(dt.dtype)
        dt[UP : UP + F, lanes] = (dv * gs).astype(dt.dtype)

    own_p = fold(nt(split3(fold(dhq[UP:FP, :])), ht[...]))
    pown[:, 0:F] = own_p + fold(erq[...].T[0:32, 0:F])
    c_py = Exchange(py_r)
    for d in (1, 3, 2):
        c_py.send(pown, py_r.at[d - 1], to_y(d))
    t1 = t_own(3, 2)

    dc[...] = dt[...].T.astype(BF)
    c_dc = send(dc, dcp, to_core)

    @pl.loop(0, 4)
    def _(i):
        w = [ws[2 * i + n // 2, :, half_lanes(core, n % 2)] for n in range(4)]
        r = nn(dc[...], jnp.concatenate(w, axis=1))
        for n in range(4):
            rsf[i, n] = r[:, n * 128 : (n + 1) * 128]

    c_w.wait_recv()
    c_dc.wait_recv()

    def rs_peer(d):
        i = wrap(x + d)
        r = nn(dcp[0:256, :], jnp.concatenate([wsp[2 * i], wsp[2 * i + 1]], axis=1))
        for n in range(4):
            v = rsf[i, n, top] + r[:, n * 128 : (n + 1) * 128]
            rsf[i, n, top] = v
            rsp[i, n, top] = v.astype(BF)
        i = wrap(z + d)
        lanes = pl.ds(pl.multiple_of(lax.rem(i, 2) * 128, 128), 128)
        w = [wsp[2 * n + i // 2, :, lanes] for n in range(4)]
        r = nn(dcp[256:512, :], jnp.concatenate(w, axis=1))
        for n in range(4):
            v = rsf[n, i, bottom] + r[:, n * 128 : (n + 1) * 128]
            rsf[n, i, bottom] = v
            rsp[n, i, bottom] = v.astype(BF)

    top, bottom = pl.ds(0, 256), pl.ds(256, 256)
    x1, x2, x3 = wrap(x + 1), wrap(x + 2), wrap(x + 3)
    z1, z2, z3 = wrap(z + 1), wrap(z + 2), wrap(z + 3)
    q0, q1, q2, q3 = (pl.ds(n * 128, 128) for n in range(4))
    c_ha, c_hb = Exchange(ha), Exchange(hb)
    c_na, c_nb = Exchange(ra.at[pl.ds(0, 2)]), Exchange(rb.at[pl.ds(0, 2)])
    c_ra, c_rb = Exchange(ra.at[pl.ds(2, 2)]), Exchange(rb.at[pl.ds(2, 2)])
    rs_peer(2)
    c_py.wait_recv()
    pf[...] = ((pown[...] + py_r[1]) + (py_r[0] + py_r[2])) * 0.25
    base = core * 48 + z * 12
    for c in range(3):
        pg[base + x * 3 + c] = pf[:, c * 128 : (c + 1) * 128]
    own = pl.ds(base + x * 3, 3)
    c_pg = Exchange(pg.at[pl.ds(0, 45)])
    for i, j in PLANE:
        c_pg.send(pg.at[own], pg.at[own], to_plane(i, j))
    c_ha.send(rsp.at[x2, :, q0], ha.at[0], to_x(1))
    c_ha.send(rsp.at[x2, :, q1], ha.at[1], to_x(3))
    c_hb.send(rsp.at[:, z2, q2], hb.at[0], to_z(1))
    c_hb.send(rsp.at[:, z2, q3], hb.at[1], to_z(3))
    p3[...] = split3(pf[...])
    hp3 = split3(fold(nn(p3[:, 0:F], ht[...])))

    def s_part(c):
        s = fold(nn(hp3, dys[c]) + nn(p3[:, 0:F], ers[c]))
        for j in range(8):
            sb[8 * c + j] = s[:, j * 128 : (j + 1) * 128]

    s_part(2 * other)
    s_part(2 * other + 1)
    c_sc = send(sb.at[pl.ds(16 * other, 16)], sc_r, to_core)
    s_part(2 * core)
    s_part(2 * core + 1)

    t0[0].wait_recv()
    far = [t_right(0, 2)]
    t0[1].wait_recv()
    far.append(t_left(2, 1))
    t2 = t_own(5, 1)

    rs_peer(1)
    rs_peer(3)
    c_sc.wait_recv()
    half = pl.ds(16 * core, 16)
    sb[half] = sb[half] + sc_r[...]
    c_sp = Exchange(sp_r)
    for i, j in PLANE:
        c_sp.send(
            sb.at[16 * core + 4 * wrap(x + i) + wrap(z + j)], sp_r.at[4 * i + j - 1], to_plane(i, j)
        )
    c_na.send(rsp.at[x1, :, q1], ra.at[0], to_x(1))
    c_na.send(rsp.at[x3, :, q0], ra.at[1], to_x(3))
    c_nb.send(rsp.at[:, z1, q3], rb.at[0], to_z(1))
    c_nb.send(rsp.at[:, z3, q2], rb.at[1], to_z(3))
    rs_peer(0)
    t1[1].wait_recv()
    far.append(t_left(3, 1))
    c_pg.wait_recv()
    own = pl.ds(core * 48, 48)
    c_pgc = send(pg.at[own], pg.at[own], to_core)
    c_ha.wait_recv()
    rsp[x1, :, q0] = (rsf[x1, :, q0] + ha[0].astype(F32)).astype(BF)
    rsp[x3, :, q1] = (rsf[x3, :, q1] + ha[1].astype(F32)).astype(BF)
    c_ra.send(rsp.at[x1, :, q0], ra.at[2], to_x(1))
    c_ra.send(rsp.at[x3, :, q1], ra.at[3], to_x(3))

    c_hb.wait_recv()
    rsp[:, z1, q2] = (rsf[:, z1, q2] + hb[0].astype(F32)).astype(BF)
    rsp[:, z3, q3] = (rsf[:, z3, q3] + hb[1].astype(F32)).astype(BF)
    c_rb.send(rsp.at[:, z1, q2], rb.at[2], to_z(1))
    c_rb.send(rsp.at[:, z3, q3], rb.at[3], to_z(3))
    c_sp.wait_recv()
    mine = core * 16 + x * 4 + z
    s2[...] = jnp.sum(sp_r[...], axis=0) + sb[mine]
    c_sy = Exchange(sy_r)
    for d in (1, 3, 2):
        c_sy.send(s2, sy_r.at[d - 1], to_y(d))
    t3, t4 = t_own(6, 1), t_own(7, 1)
    c_pgc.wait_recv()
    for i in range(12):
        ct[:, i] = jnp.transpose(pg[8 * i : 8 * i + 8], (1, 0, 2))
    lane = lax.broadcasted_iota(jnp.int32, (1, 128), 1)
    done_b, done_t = [], []

    def total(v):
        v = jnp.sum(v, axis=0)
        return jnp.sum(jnp.sum(v, axis=0, keepdims=True), axis=1, keepdims=True)

    for k in range(R):
        v = ct[k]
        t = jnp.where(lane == k, 1.0, 0.0)
        coeffs = [total(b * v) for b in done_b]
        for c, b, tb in zip(coeffs, done_b, done_t):
            v = v - c[None] * b
            t = t - c * tb
        scale = lax.rsqrt(total(v * v) + 1e-06)
        done_b.append(v * scale[None])
        done_t.append(t * scale)
        tt[k : k + 1, :] = done_t[-1]

    def m_part(k):
        ms[k] = nn(ht[...], dys[k]) + ers[k].astype(F32)

    pl.loop(0, 2)(m_part)
    far.append(t_left(4, 1))
    t2[0].wait_recv()
    far.append(t_right(5, 1))
    c_sy.wait_recv()
    s = (s2[...] + sy_r[1]) + (sy_r[0] + sy_r[2])
    q = jnp.zeros((R, 128), F32)
    for i in range(R):
        q += tt[:, i : i + 1] * s[i : i + 1, :]
    sf[mine] = q * 0.25
    c_g = Exchange(sf.at[pl.ds(0, 15)])
    for i, j in PLANE:
        c_g.send(sf.at[mine], sf.at[mine], to_plane(i, j))

    c_zx = Exchange(zx)

    def a_sum(n, lo, hi, j):
        return rsf[x, j, pl.ds(n * 128, 128)] + (ra[lo, j].astype(F32) + ra[hi, j].astype(F32))

    def b_sum(n, lo, hi, j):
        return rsf[j, z, pl.ds(n * 128, 128)] + (rb[lo, j].astype(F32) + rb[hi, j].astype(F32))

    c_na.wait_recv()
    c_ra.wait_recv()
    for j in (1, 3, 2):
        zj = wrap(z + j)
        a1[j, q0] = a_sum(0, 2, 1, zj).astype(BF)
        a1[j, q1] = a_sum(1, 0, 3, zj).astype(BF)
        c_zx.send(a1.at[j], zx.at[j - 1], to_z(j))
    c_nb.wait_recv()
    c_rb.wait_recv()
    for j in (1, 3, 2):
        xj = wrap(x + j)
        b1[j, q0] = b_sum(2, 2, 1, xj).astype(BF)
        b1[j, q1] = b_sum(3, 0, 3, xj).astype(BF)
        c_zx.send(b1.at[j], zx.at[j + 2], to_x(j))
    pl.loop(2, 4)(m_part)
    t3[1].wait_recv()
    far.append(t_left(6, 1))
    t4[0].wait_recv()
    far.append(t_right(7, 1))
    p = jnp.zeros((R, FP), F32)
    for i in range(R):
        p += tt[:, i : i + 1] * pf[i : i + 1, :]
    hi, mid, low = parts(p)
    rows = [hi, hi, mid, hi, low, mid] + [jnp.zeros_like(p)] * 10
    left[...] = jnp.concatenate(rows, axis=0).T.astype(BF)
    right[48:128, :] = jnp.zeros((80, D), BF)

    def right_part(b):
        hi, mid, low = parts(sf[b])
        r = jnp.concatenate([hi, mid, hi, low, hi, mid], axis=0).astype(BF)
        right[0:48, pl.ds(pl.multiple_of(b * 128, 128), 128)] = r

    c_g.wait_recv()
    own = pl.ds(core * 16, 16)
    c_gc = send(sf.at[own], sf.at[own], to_core)
    for i in range(16):
        right_part(core * 16 + i)
    def finals(j):
        block, lo = j // 2, pl.multiple_of(lax.rem(j, 2) * 512, 512)
        cols = pl.ds(pl.multiple_of(j * 512, 512), 512)
        approx = nn(left[0:F, :], right[:, cols])
        ne[:, cols] = (ms[block, :, pl.ds(lo, 512)] - approx).astype(BF)
    @pl.loop(0, 4)
    def _(j):
        finals(core * 4 + j)

    a = jnp.concatenate([a_sum(0, 2, 1, z), a_sum(1, 0, 3, z)], axis=0)
    b = jnp.concatenate([b_sum(2, 2, 1, x), b_sum(3, 0, 3, x)], axis=0)
    c_gc.wait_recv()
    for i in range(16):
        right_part(other * 16 + i)
    c_zx.wait_recv()
    for d in range(3):
        a += zx[d].astype(F32)
        b += zx[d + 3].astype(F32)
    igs[0:256, :] = a.astype(BF)
    igs[256:512, :] = b.astype(BF)
    for c in (t1[0], t2[1], t3[0], t4[1], *far):
        c.wait_recv()
    for c in sent:
        c.wait_send()


def exchange(x, dy, wg, wu, wd, er, mo, q):
    v = pltpu.VMEM
    any_spec = pl.BlockSpec(memory_space=pl.ANY)
    vmem_spec = pl.BlockSpec(memory_space=pltpu.VMEM)
    scratch = [
        v((8, TOK, 512), BF), v((NK, TOK, KC), BF), v((8, KP, 512), BF),
        v((NK, FP, KC), BF), v((NK, F, KC), BF), v((R, D), F32), v((8, KP, 256), BF),
        v((704, TOK), F32), v((FP, TOK), F32), v((F, TOK), BF), v((KP, TOK), F32),
        v((TOK, KP), BF), v((TOK, KP), BF), v((FP, 128), F32),
        v((R, FP), F32), v((3, R, FP), F32), v((32, FP), BF), v((R, FP), F32),
        v((96, 8, 128), F32), v((8, 12, 8, 128), F32), v((8, 128), F32),
        v((32, 8, 128), F32), v((16, 8, 128), F32), v((15, 8, 128), F32),
        v((8, 128), F32), v((3, 8, 128), F32), v((32, 8, 128), F32),
        v((4, 4, TOK, 128), F32), v((4, 4, TOK, 128), BF),
        v((2, 4, 128, 128), BF), v((2, 4, 128, 128), BF),
        v((4, 4, 128, 128), BF), v((4, 4, 128, 128), BF),
        v((4, 256, 128), BF), v((4, 256, 128), BF), v((6, 256, 128), BF),
        pltpu.SemaphoreType.DMA((21,)),
        pltpu.SemaphoreType.DMA((N_SEM,)),
        pltpu.SemaphoreType.DMA((N_SEM,)),
    ]
    out_shape = (
        v((TOK, 128), BF), v((F, D), BF), v((4, 8, F, 128), BF),
        v((NK, F, KC), F32), v((F, KC), F32), v((FP, 128), BF), v((128, D), BF),
    )
    return pl.pallas_call(
        step_kernel,
        out_shape=out_shape,
        in_specs=[any_spec] * 8,
        out_specs=[vmem_spec] * 7,
        scratch_shapes=scratch,
        compiler_params=pltpu.CompilerParams(
            collective_id=0, has_side_effects=True, vmem_limit_bytes=42 * 1024 * 1024
        ),
        name="exchange",
    )(x, dy, wg, wu, wd, er, mo, q)


def store_kernel(
    ig, ne, tg, ms, mos, left, right, ig_o, nd_o, ne_o, nm_o, nd, ne2, nm, sem
):
    dp = lax.axis_index("dp")
    core = lax.rem(lax.axis_index("mp"), 2)
    copies = []

    def out(src, dst):
        copies.append(pltpu.make_async_copy(src, dst, sem.at[len(copies)]))
        copies[-1].start()

    def at(block, n):
        return pl.ds(pl.multiple_of(block * 512, 512), n * 512)

    for n in range(2):
        cols = at(core * 4 + 2 * n, 2)
        out(ne.at[:, cols], ne_o.at[:, cols])
    out(ig, ig_o)
    factor = left[0:F, :]
    for j in range(8):
        block = (1 - core) * 4 + j if j < 4 else core * 4 + j - 4
        chunk = (1 - core) * 2 + j // 2 if j < 4 else core * 2 + (j - 4) // 2
        approx = nn(factor, right[:, at(block, 1)])
        cols = slice(j * 512, (j + 1) * 512)
        half = slice((j % 2) * 512, (j % 2 + 1) * 512)
        if j < 4:
            ne2[:, cols] = (ms[chunk, :, half] - approx).astype(BF)
            out(ne2.at[:, cols], ne_o.at[:, at(block, 1)])
        for c in range(4):
            t = tg[chunk, (j % 2) * 4 + c].astype(F32)
            nd[:, j * 512 + c * 128 : j * 512 + (c + 1) * 128] = (
                t - 0.1 * approx[:, c * 128 : (c + 1) * 128]
            ).astype(BF)
        out(nd.at[:, cols], nd_o.at[:, at(block, 1)])
        if j < 2:
            cols = slice(j * 512, (j + 1) * 512)
            nm[:, cols] = 0.9 * mos[:, cols] + nn(factor, right[:, at(2 * dp + j, 1)])
            out(nm.at[:, cols], nm_o.at[:, cols])
    for c in copies:
        c.wait()


def store(*args):
    v = pltpu.VMEM
    args = [pltpu.with_memory_space_constraint(a, pltpu.VMEM) for a in args]
    return pl.pallas_call(
        store_kernel,
        out_shape=(
            jax.ShapeDtypeStruct((TOK, 128), BF),
            jax.ShapeDtypeStruct((F, D), BF),
            jax.ShapeDtypeStruct((F, D), BF),
            jax.ShapeDtypeStruct((F, KC), F32),
        ),
        in_specs=[pl.BlockSpec(memory_space=pltpu.VMEM)] * len(args),
        out_specs=[pl.BlockSpec(memory_space=pl.ANY)] * 4,
        scratch_shapes=[
            v((F, D), BF), v((F, D // 2), BF), v((F, KC), F32), pltpu.SemaphoreType.DMA((17,)),
        ],
        compiler_params=pltpu.CompilerParams(vmem_limit_bytes=20 * 1024 * 1024),
        name="store",
    )(*args)


def body(inputs, out_grads, w_gate, w_up, w_down, err_down, mom_down, q_down):
    kept = exchange(
        inputs, out_grads, w_gate.T, w_up.T, w_down, err_down[0], mom_down, q_down.T
    )
    ig, nd, ne, nm = store(*kept)
    return ig, nd, ne[None], nm


def solution(mesh):
    in_specs = (
        P("dp", None), P("dp", None), P(None, "mp"), P(None, "mp"), P("mp", None),
        P("dp", "mp", None), P("mp", "dp"), P(),
    )
    out_specs = (P("dp", "mp"), P("mp", None), P("dp", "mp", None), P("mp", "dp"))
    return jax.shard_map(body, mesh=mesh, in_specs=in_specs, out_specs=out_specs, check_vma=False)
```

```python
import jax
import jax.numpy as jnp
from jax import lax
from jax.experimental import pallas as pl
from jax.experimental.pallas import tpu as pltpu
from jax.sharding import PartitionSpec as P

MESH = pl.DeviceIdType.MESH
BF = jnp.bfloat16
F32 = jnp.float32
TOK, D, F, FP, R = 512, 4096, 344, 384, 8
UP = 352
KP = 768
KC = 1024
NK = D // KC
N_SEM = 34
PLANE = [(i, j) for i in range(4) for j in range(4) if i or j]


def nt(a, b):
    return lax.dot_general(a, b, (((1,), (1,)), ((), ())), preferred_element_type=F32)


def nn(a, b):
    return lax.dot_general(a, b, (((1,), (0,)), ((), ())), preferred_element_type=F32)


def parts(v):
    hi = v.astype(BF).astype(F32)
    rest = v - hi
    mid = rest.astype(BF).astype(F32)
    return hi, mid, rest - mid


def split3(v):
    hi, mid, low = parts(v)
    return jnp.concatenate([hi, mid, low, jnp.zeros_like(v)], axis=0).astype(BF)


def fold(r):
    return (r[0:8] + r[8:16]) + r[16:24]


def wrap(v):
    return lax.rem(v, 4)


def step_kernel(
    x_h, dy_h, wg_h, wu_h, wd_h, er_h, mo_h, q_h,
    igs, tg, ms, mos, left, right,
    xs, dys, ws, wds, ers, qs, wsp,
    gu, dhq, ht, dt, dc, dcp, erq,
    pown, py_r, p3, pf, pg, ct, tt,
    sb, sc_r, sp_r, s2, sy_r, sf,
    rsf, rsp, ha, hb, ra, rb, a1, b1, zx,
    load_sem, send_sem, recv_sem,
):
    dp = lax.axis_index("dp")
    mp = lax.axis_index("mp")
    core = lax.rem(mp, 2)
    z = lax.rem(mp // 2, 4)
    x = mp // 8
    other = 1 - core
    to_core = (dp, mp + 1 - 2 * core)

    def to_x(d):
        return (dp, wrap(x + d) * 8 + z * 2 + core)

    def to_z(d):
        return (dp, x * 8 + wrap(z + d) * 2 + core)

    def to_y(d):
        return (wrap(dp + d), mp)

    def to_plane(i, j):
        return (dp, wrap(x + i) * 8 + wrap(z + j) * 2 + core)

    barrier = pltpu.get_barrier_semaphore()
    peers = [to_core] + [to_plane(i, j) for i, j in PLANE] + [to_y(d) for d in (1, 2, 3)]
    for peer in peers:
        pl.semaphore_signal(barrier, inc=1, device_id=peer, device_id_type=MESH)

    def group(k):
        return k if k < 2 else 1 + k // 2

    def lx(k):
        cols = pl.ds(k * 512, 512)
        return pltpu.make_async_copy(x_h.at[:, cols], xs.at[k], load_sem.at[group(k)])

    def lwg(k):
        cols = pl.ds(k * 512, 512)
        return pltpu.make_async_copy(wg_h.at[:, cols], ws.at[k, pl.ds(0, F)], load_sem.at[5 + group(k)])

    def lwu(k):
        cols = pl.ds(k * 512, 512)
        return pltpu.make_async_copy(wu_h.at[:, cols], ws.at[k, pl.ds(UP, F)], load_sem.at[5 + group(k)])

    def arrived(k, n, sem):
        at = xs.at[pl.ds(k, n)]
        pltpu.make_async_copy(at, at, load_sem.at[sem]).wait()
        at = ws.at[pl.ds(k, n), pl.ds(0, 2 * F)]
        pltpu.make_async_copy(at, at, load_sem.at[5 + sem]).wait()

    def ly(k):
        return pltpu.make_async_copy(dy_h.at[:, pl.ds(k * KC, KC)], dys.at[k], load_sem.at[10 + k])

    def lwd(k):
        return pltpu.make_async_copy(
            wd_h.at[:, pl.ds(k * KC, KC)], wds.at[k, pl.ds(0, F)], load_sem.at[14 + k]
        )

    def ler(k):
        return pltpu.make_async_copy(er_h.at[:, pl.ds(k * KC, KC)], ers.at[k], load_sem.at[18])

    lmo = pltpu.make_async_copy(mo_h, mos, load_sem.at[19])
    lq = pltpu.make_async_copy(q_h, qs, load_sem.at[20])
    for k in range(8):
        lx(k).start()
        lwg(k).start()
        lwu(k).start()
        if k == 3:
            lmo.start()
            lwd(dp).start()
    lq.start()
    ly(dp).start()
    for i in range(1, NK):
        ly(wrap(dp + i)).start()
        lwd(wrap(dp + i)).start()
    for k in range(NK):
        ler(k).start()

    count = [0]
    sent = []

    class Exchange:
        def __init__(self, whole):
            i = count[0]
            count[0] += 1
            self.sems = send_sem.at[i], recv_sem.at[i]
            self.whole = whole
            sent.append(self)

        def send(self, src, dst, device):
            pltpu.make_async_remote_copy(
                src_ref=src, dst_ref=dst, send_sem=self.sems[0], recv_sem=self.sems[1],
                device_id=device, device_id_type=MESH,
            ).start()
            return self

        def wait_send(self):
            pltpu.make_async_copy(self.whole, self.whole, self.sems[0]).wait()

        def wait_recv(self):
            pltpu.make_async_copy(self.whole, self.whole, self.sems[1]).wait()

    def send(src, dst, device):
        return Exchange(dst).send(src, dst, device)

    for ref in (gu, dhq, erq, pown):
        ref[...] = jnp.zeros_like(ref)
    ws[:, F:UP, :] = jnp.zeros((8, UP - F, 512), BF)
    ws[:, UP + F :, :] = jnp.zeros((8, KP - UP - F, 512), BF)
    wds[:, F:UP, :] = jnp.zeros((NK, UP - F, KC), BF)
    dt[F:UP, :] = jnp.zeros((UP - F, TOK), dt.dtype)
    dt[UP + F :, :] = jnp.zeros((KP - UP - F, TOK), dt.dtype)

    @pl.loop(0, 2)
    def _(k):
        arrived(k, 1, k)
        gu[...] += nt(ws[k, 0:704], xs[k])

    def gate_up(k):
        arrived(2 * k, 2, 1 + k)
        w = jnp.concatenate([ws[2 * k, 0:704], ws[2 * k + 1, 0:704]], axis=1)
        gu[...] += nt(w, jnp.concatenate([xs[2 * k], xs[2 * k + 1]], axis=1))

    pl.loop(1, 2)(gate_up)
    pl.semaphore_wait(barrier, len(peers))
    lmo.wait()
    lwd(dp).wait()
    for p in range(8):
        lanes = pl.ds(p * 128, 128)
        tg[dp, p] = (wds[dp, 0:F, lanes].astype(F32) - 0.1 * (0.9 * mos[:, lanes])).astype(BF)
    y_right, y_left = wrap(dp + 1), wrap(dp + 3)

    def t_own(lo, n):
        at = tg.at[dp, pl.ds(lo, n)]
        return send(at, at, to_y(1)), send(at, at, to_y(3))

    def t_right(lo, n):
        at = tg.at[y_left, pl.ds(lo, n)]
        return send(at, at, to_y(1))

    def t_left(lo, n):
        at = tg.at[y_right, pl.ds(lo, n)]
        return send(at, at, to_y(3))

    t0 = t_own(0, 3)

    pl.loop(2, 4)(gate_up)

    def half_lanes(c, n):
        return pl.ds(pl.multiple_of(c * 128 + n * 256, 128), 128)

    c_w = Exchange(wsp)
    for n in range(2):
        c_w.send(ws.at[:, :, half_lanes(other, n)], wsp.at[:, :, pl.ds(n * 128, 128)], to_core)

    lq.wait()
    for k in range(NK):
        wds[k, UP:FP, :] = split3(qs[:, k * KC : (k + 1) * KC])

    @pl.loop(0, 2)
    def _(i):
        k, n = wrap(dp + 2 * i), wrap(dp + 2 * i + 1)
        ly(k).wait()
        ly(n).wait()
        lwd(n).wait()

        @pl.when(i > 0)
        def _():
            lwd(k).wait()

        dhq[...] += nt(
            jnp.concatenate([wds[k], wds[n]], axis=1), jnp.concatenate([dys[k], dys[n]], axis=1)
        )

    pltpu.make_async_copy(er_h, er_h, load_sem.at[18]).wait()
    erq[0:F, 0:32] = nt(
        jnp.concatenate([ers[k] for k in range(NK)], axis=1),
        jnp.concatenate([wds[k, UP:FP, :] for k in range(NK)], axis=1),
    )

    @pl.loop(0, 4)
    def _(i):
        lanes = pl.ds(pl.multiple_of(i * 128, 128), 128)
        gv, uv, dv = gu[0:F, lanes], gu[UP : UP + F, lanes], dhq[0:F, lanes]
        sig = jax.nn.sigmoid(gv)
        gs = gv * sig
        ht[:, lanes] = (gs * uv).astype(BF)
        dt[0:F, lanes] = (dv * uv * sig * (1.0 + gv * (1.0 - sig))).astype(dt.dtype)
        dt[UP : UP + F, lanes] = (dv * gs).astype(dt.dtype)

    own_p = fold(nt(split3(fold(dhq[UP:FP, :])), ht[...]))
    pown[:, 0:F] = own_p + fold(erq[...].T[0:32, 0:F])
    c_py = Exchange(py_r)
    for d in (1, 3, 2):
        c_py.send(pown, py_r.at[d - 1], to_y(d))
    t1 = t_own(3, 2)

    dc[...] = dt[...].T.astype(BF)
    c_dc = send(dc, dcp, to_core)

    @pl.loop(0, 4)
    def _(i):
        w = [ws[2 * i + n // 2, :, half_lanes(core, n % 2)] for n in range(4)]
        r = nn(dc[...], jnp.concatenate(w, axis=1))
        for n in range(4):
            rsf[i, n] = r[:, n * 128 : (n + 1) * 128]

    c_w.wait_recv()
    c_dc.wait_recv()

    def rs_peer(d):
        i = wrap(x + d)
        r = nn(dcp[0:256, :], jnp.concatenate([wsp[2 * i], wsp[2 * i + 1]], axis=1))
        for n in range(4):
            v = rsf[i, n, top] + r[:, n * 128 : (n + 1) * 128]
            rsf[i, n, top] = v
            rsp[i, n, top] = v.astype(BF)
        i = wrap(z + d)
        lanes = pl.ds(pl.multiple_of(lax.rem(i, 2) * 128, 128), 128)
        w = [wsp[2 * n + i // 2, :, lanes] for n in range(4)]
        r = nn(dcp[256:512, :], jnp.concatenate(w, axis=1))
        for n in range(4):
            v = rsf[n, i, bottom] + r[:, n * 128 : (n + 1) * 128]
            rsf[n, i, bottom] = v
            rsp[n, i, bottom] = v.astype(BF)

    top, bottom = pl.ds(0, 256), pl.ds(256, 256)
    x1, x2, x3 = wrap(x + 1), wrap(x + 2), wrap(x + 3)
    z1, z2, z3 = wrap(z + 1), wrap(z + 2), wrap(z + 3)
    q0, q1, q2, q3 = (pl.ds(n * 128, 128) for n in range(4))
    c_ha, c_hb = Exchange(ha), Exchange(hb)
    c_na, c_nb = Exchange(ra.at[pl.ds(0, 2)]), Exchange(rb.at[pl.ds(0, 2)])
    c_ra, c_rb = Exchange(ra.at[pl.ds(2, 2)]), Exchange(rb.at[pl.ds(2, 2)])
    rs_peer(2)
    c_py.wait_recv()
    pf[...] = ((pown[...] + py_r[1]) + (py_r[0] + py_r[2])) * 0.25
    base = core * 48 + z * 12
    for c in range(3):
        pg[base + x * 3 + c] = pf[:, c * 128 : (c + 1) * 128]
    own = pl.ds(base + x * 3, 3)
    c_pg = Exchange(pg.at[pl.ds(0, 45)])
    for i, j in PLANE:
        c_pg.send(pg.at[own], pg.at[own], to_plane(i, j))
    c_ha.send(rsp.at[x2, :, q0], ha.at[0], to_x(1))
    c_ha.send(rsp.at[x2, :, q1], ha.at[1], to_x(3))
    c_hb.send(rsp.at[:, z2, q2], hb.at[0], to_z(1))
    c_hb.send(rsp.at[:, z2, q3], hb.at[1], to_z(3))
    p3[...] = split3(pf[...])
    hp3 = split3(fold(nn(p3[:, 0:F], ht[...])))

    def s_part(c):
        s = fold(nn(hp3, dys[c]) + nn(p3[:, 0:F], ers[c]))
        for j in range(8):
            sb[8 * c + j] = s[:, j * 128 : (j + 1) * 128]

    s_part(2 * other)
    s_part(2 * other + 1)
    c_sc = send(sb.at[pl.ds(16 * other, 16)], sc_r, to_core)
    s_part(2 * core)
    s_part(2 * core + 1)

    t0[0].wait_recv()
    far = [t_right(0, 2)]
    t0[1].wait_recv()
    far.append(t_left(2, 1))
    t2 = t_own(5, 1)

    rs_peer(1)
    rs_peer(3)
    c_sc.wait_recv()
    half = pl.ds(16 * core, 16)
    sb[half] = sb[half] + sc_r[...]
    c_sp = Exchange(sp_r)
    for i, j in PLANE:
        c_sp.send(
            sb.at[16 * core + 4 * wrap(x + i) + wrap(z + j)], sp_r.at[4 * i + j - 1], to_plane(i, j)
        )
    c_na.send(rsp.at[x1, :, q1], ra.at[0], to_x(1))
    c_na.send(rsp.at[x3, :, q0], ra.at[1], to_x(3))
    c_nb.send(rsp.at[:, z1, q3], rb.at[0], to_z(1))
    c_nb.send(rsp.at[:, z3, q2], rb.at[1], to_z(3))
    rs_peer(0)
    t1[1].wait_recv()
    far.append(t_left(3, 1))
    c_pg.wait_recv()
    own = pl.ds(core * 48, 48)
    c_pgc = send(pg.at[own], pg.at[own], to_core)
    c_ha.wait_recv()
    rsp[x1, :, q0] = (rsf[x1, :, q0] + ha[0].astype(F32)).astype(BF)
    rsp[x3, :, q1] = (rsf[x3, :, q1] + ha[1].astype(F32)).astype(BF)
    c_ra.send(rsp.at[x1, :, q0], ra.at[2], to_x(1))
    c_ra.send(rsp.at[x3, :, q1], ra.at[3], to_x(3))

    c_hb.wait_recv()
    rsp[:, z1, q2] = (rsf[:, z1, q2] + hb[0].astype(F32)).astype(BF)
    rsp[:, z3, q3] = (rsf[:, z3, q3] + hb[1].astype(F32)).astype(BF)
    c_rb.send(rsp.at[:, z1, q2], rb.at[2], to_z(1))
    c_rb.send(rsp.at[:, z3, q3], rb.at[3], to_z(3))
    c_sp.wait_recv()
    mine = core * 16 + x * 4 + z
    s2[...] = jnp.sum(sp_r[...], axis=0) + sb[mine]
    c_sy = Exchange(sy_r)
    for d in (1, 3, 2):
        c_sy.send(s2, sy_r.at[d - 1], to_y(d))
    t3, t4 = t_own(6, 1), t_own(7, 1)
    c_pgc.wait_recv()
    for i in range(12):
        ct[:, i] = jnp.transpose(pg[8 * i : 8 * i + 8], (1, 0, 2))
    lane = lax.broadcasted_iota(jnp.int32, (1, 128), 1)
    done_b, done_t = [], []

    def total(v):
        v = jnp.sum(v, axis=0)
        return jnp.sum(jnp.sum(v, axis=0, keepdims=True), axis=1, keepdims=True)

    for k in range(R):
        v = ct[k]
        t = jnp.where(lane == k, 1.0, 0.0)
        coeffs = [total(b * v) for b in done_b]
        for c, b, tb in zip(coeffs, done_b, done_t):
            v = v - c[None] * b
            t = t - c * tb
        scale = lax.rsqrt(total(v * v) + 1e-06)
        done_b.append(v * scale[None])
        done_t.append(t * scale)
        tt[k : k + 1, :] = done_t[-1]

    def m_part(k):
        ms[k] = nn(ht[...], dys[k]) + ers[k].astype(F32)

    pl.loop(0, 2)(m_part)
    far.append(t_left(4, 1))
    t2[0].wait_recv()
    far.append(t_right(5, 1))
    c_sy.wait_recv()
    s = (s2[...] + sy_r[1]) + (sy_r[0] + sy_r[2])
    q = jnp.zeros((R, 128), F32)
    for i in range(R):
        q += tt[:, i : i + 1] * s[i : i + 1, :]
    sf[mine] = q * 0.25
    c_g = Exchange(sf.at[pl.ds(0, 15)])
    for i, j in PLANE:
        c_g.send(sf.at[mine], sf.at[mine], to_plane(i, j))

    c_zx = Exchange(zx)

    def a_sum(n, lo, hi, j):
        return rsf[x, j, pl.ds(n * 128, 128)] + (ra[lo, j].astype(F32) + ra[hi, j].astype(F32))

    def b_sum(n, lo, hi, j):
        return rsf[j, z, pl.ds(n * 128, 128)] + (rb[lo, j].astype(F32) + rb[hi, j].astype(F32))

    c_na.wait_recv()
    c_ra.wait_recv()
    for j in (1, 3, 2):
        zj = wrap(z + j)
        a1[j, q0] = a_sum(0, 2, 1, zj).astype(BF)
        a1[j, q1] = a_sum(1, 0, 3, zj).astype(BF)
        c_zx.send(a1.at[j], zx.at[j - 1], to_z(j))
    c_nb.wait_recv()
    c_rb.wait_recv()
    for j in (1, 3, 2):
        xj = wrap(x + j)
        b1[j, q0] = b_sum(2, 2, 1, xj).astype(BF)
        b1[j, q1] = b_sum(3, 0, 3, xj).astype(BF)
        c_zx.send(b1.at[j], zx.at[j + 2], to_x(j))
    pl.loop(2, 4)(m_part)
    t3[1].wait_recv()
    far.append(t_left(6, 1))
    t4[0].wait_recv()
    far.append(t_right(7, 1))
    p = jnp.zeros((R, FP), F32)
    for i in range(R):
        p += tt[:, i : i + 1] * pf[i : i + 1, :]
    hi, mid, low = parts(p)
    rows = [hi, hi, mid, hi, low, mid] + [jnp.zeros_like(p)] * 10
    left[...] = jnp.concatenate(rows, axis=0).T.astype(BF)
    right[48:128, :] = jnp.zeros((80, D), BF)

    def right_part(b):
        hi, mid, low = parts(sf[b])
        r = jnp.concatenate([hi, mid, hi, low, hi, mid], axis=0).astype(BF)
        right[0:48, pl.ds(pl.multiple_of(b * 128, 128), 128)] = r

    c_g.wait_recv()
    own = pl.ds(core * 16, 16)
    c_gc = send(sf.at[own], sf.at[own], to_core)
    for i in range(16):
        right_part(core * 16 + i)
    a = jnp.concatenate([a_sum(0, 2, 1, z), a_sum(1, 0, 3, z)], axis=0)
    b = jnp.concatenate([b_sum(2, 2, 1, x), b_sum(3, 0, 3, x)], axis=0)
    c_gc.wait_recv()
    for i in range(16):
        right_part(other * 16 + i)
    c_zx.wait_recv()
    for d in range(3):
        a += zx[d].astype(F32)
        b += zx[d + 3].astype(F32)
    igs[0:256, :] = a.astype(BF)
    igs[256:512, :] = b.astype(BF)
    for c in (t1[0], t2[1], t3[0], t4[1], *far):
        c.wait_recv()
    for c in sent:
        c.wait_send()


def exchange(x, dy, wg, wu, wd, er, mo, q):
    v = pltpu.VMEM
    any_spec = pl.BlockSpec(memory_space=pl.ANY)
    vmem_spec = pl.BlockSpec(memory_space=pltpu.VMEM)
    scratch = [
        v((8, TOK, 512), BF), v((NK, TOK, KC), BF), v((8, KP, 512), BF),
        v((NK, FP, KC), BF), v((NK, F, KC), BF), v((R, D), F32), v((8, KP, 256), BF),
        v((704, TOK), F32), v((FP, TOK), F32), v((F, TOK), BF), v((KP, TOK), F32),
        v((TOK, KP), BF), v((TOK, KP), BF), v((FP, 128), F32),
        v((R, FP), F32), v((3, R, FP), F32), v((32, FP), BF), v((R, FP), F32),
        v((96, 8, 128), F32), v((8, 12, 8, 128), F32), v((8, 128), F32),
        v((32, 8, 128), F32), v((16, 8, 128), F32), v((15, 8, 128), F32),
        v((8, 128), F32), v((3, 8, 128), F32), v((32, 8, 128), F32),
        v((4, 4, TOK, 128), F32), v((4, 4, TOK, 128), BF),
        v((2, 4, 128, 128), BF), v((2, 4, 128, 128), BF),
        v((4, 4, 128, 128), BF), v((4, 4, 128, 128), BF),
        v((4, 256, 128), BF), v((4, 256, 128), BF), v((6, 256, 128), BF),
        pltpu.SemaphoreType.DMA((21,)),
        pltpu.SemaphoreType.DMA((N_SEM,)),
        pltpu.SemaphoreType.DMA((N_SEM,)),
    ]
    out_shape = (
        v((TOK, 128), BF), v((4, 8, F, 128), BF),
        v((NK, F, KC), F32), v((F, KC), F32), v((FP, 128), BF), v((128, D), BF),
    )
    return pl.pallas_call(
        step_kernel,
        out_shape=out_shape,
        in_specs=[any_spec] * 8,
        out_specs=[vmem_spec] * 6,
        scratch_shapes=scratch,
        compiler_params=pltpu.CompilerParams(
            collective_id=0, has_side_effects=True, vmem_limit_bytes=42 * 1024 * 1024
        ),
        name="exchange",
    )(x, dy, wg, wu, wd, er, mo, q)


def store_kernel(
    ig, tg, ms, mos, left, right, ig_o, nd_o, ne_o, nm_o, nd, ne, nm, sem
):
    dp = lax.axis_index("dp")
    copies = []

    def out(src, dst):
        copies.append(pltpu.make_async_copy(src, dst, sem.at[len(copies)]))
        copies[-1].start()

    out(ig, ig_o)
    factor = left[0:F, :]
    for j in range(8):
        cols = slice(j * 512, (j + 1) * 512)
        approx = nn(factor, right[:, cols])
        ne[:, cols] = (ms[j // 2, :, (j % 2) * 512 : (j % 2 + 1) * 512] - approx).astype(BF)
        out(ne.at[:, cols], ne_o.at[:, cols])
        for c in range(4):
            t = tg[j // 2, (j % 2) * 4 + c].astype(F32)
            nd[:, j * 512 + c * 128 : j * 512 + (c + 1) * 128] = (
                t - 0.1 * approx[:, c * 128 : (c + 1) * 128]
            ).astype(BF)
        out(nd.at[:, cols], nd_o.at[:, cols])
        if j < 2:
            own = pl.ds(pl.multiple_of(dp * KC + j * 512, 512), 512)
            nm[:, cols] = 0.9 * mos[:, cols] + nn(factor, right[:, own])
            out(nm.at[:, cols], nm_o.at[:, cols])
    for c in copies:
        c.wait()


def store(*args):
    v = pltpu.VMEM
    args = [pltpu.with_memory_space_constraint(a, pltpu.VMEM) for a in args]
    return pl.pallas_call(
        store_kernel,
        out_shape=(
            jax.ShapeDtypeStruct((TOK, 128), BF),
            jax.ShapeDtypeStruct((F, D), BF),
            jax.ShapeDtypeStruct((F, D), BF),
            jax.ShapeDtypeStruct((F, KC), F32),
        ),
        in_specs=[pl.BlockSpec(memory_space=pltpu.VMEM)] * len(args),
        out_specs=[pl.BlockSpec(memory_space=pl.ANY)] * 4,
        scratch_shapes=[
            v((F, D), BF), v((F, D), BF), v((F, KC), F32), pltpu.SemaphoreType.DMA((19,)),
        ],
        compiler_params=pltpu.CompilerParams(vmem_limit_bytes=20 * 1024 * 1024),
        name="store",
    )(*args)


def body(inputs, out_grads, w_gate, w_up, w_down, err_down, mom_down, q_down):
    kept = exchange(
        inputs, out_grads, w_gate.T, w_up.T, w_down, err_down[0], mom_down, q_down.T
    )
    ig, nd, ne, nm = store(*kept)
    return ig, nd, ne[None], nm


def solution(mesh):
    in_specs = (
        P("dp", None), P("dp", None), P(None, "mp"), P(None, "mp"), P("mp", None),
        P("dp", "mp", None), P("mp", "dp"), P(),
    )
    out_specs = (P("dp", "mp"), P("mp", None), P("dp", "mp", None), P("mp", "dp"))
    return jax.shard_map(body, mesh=mesh, in_specs=in_specs, out_specs=out_specs, check_vma=False)
```
